32 devices in a mesh: sub: 4 (over x, core), beam: 4 (over z), comp: 2 (over y).
Axes of the slice: x: 2, y: 2, z: 4, core: 2. Of those that a mesh axis runs over, the one named last changes fastest.
Arguments:
- raw_pulses: bfloat16 [4096, 2, 16384], P(('sub', 'beam', 'comp')), may hold values from -6 to 6
- range_filter: float32 [2, 16384], replicated, may hold values from -4 to 4
- steer_angle: float32 [64, 4096], P(None, ('sub', 'beam', 'comp')), may hold values from -3.140625 to 3.140625
- band_offsets: int32 [2, 384], P(None, ('beam', 'comp')), may hold values from -4 to 12, as said below
- band_weights: float32 [2, 384, 8], P(None, ('beam', 'comp')), may hold values from -1.5 to 1.5
- beam_delay: float32 [2, 384], P(None, ('beam', 'comp')), may hold values from -3 to 3
Outputs:
- scene_beams: float32 [256, 2, 16384], P(('beam', 'comp'), None, 'sub')
The draws below stay inside these ranges and needn't reach their ends.
Inputs may be any that keep to these rules, and one draw needn't show every extreme that they name: `band_offsets`: for new beam u of a merge level l and a block (0 <= u < 2 * 8 2^l), each side's offset is u // 2 - 8 // 2 + 1 or one less; the first beam of every level and block takes the lesser value, the last the greater.
All inputs are finite; a program needn't handle non-finite values.
Results may differ from the reference program's by a relative error of at most 0.0059.
Values may be sent and summed in bfloat16 or wider, within the bound.
A program may use at most 128 MiB of HBM per device.

```python
import math
import jax
import jax.numpy as jnp
from jax import lax

NR = 16384
RADIX = 128
NB0 = 8
BAND = 8
PDEV = 128
PSUB = 1024
PULSES = 4096
NBT0 = 64
NEWL = 48
LEVELS = 2
N_SUB = 4
N_BEAM = 4
N_COMP = 2


def draw_band_offsets(key, part):
    blocks = N_BEAM * N_COMP
    centers = []
    first_flags = []
    last_flags = []
    for level_index in range(LEVELS):
        new_beams = 2 * NB0 * 2 ** level_index
        local_beam = jnp.arange(new_beams, dtype=jnp.int32)
        centers.append(local_beam // 2 - BAND // 2 + 1)
        first_flags.append(local_beam == 0)
        last_flags.append(local_beam == new_beams - 1)
    center_row = jnp.concatenate(centers)
    first_row = jnp.concatenate(first_flags)
    last_row = jnp.concatenate(last_flags)
    coin_flip = jax.random.randint(key, (2, blocks, NEWL), 0, 2, dtype=jnp.int32)
    lowered = jnp.where(first_row[None, None, :], 1, jnp.where(last_row[None, None, :], 0, coin_flip))
    return (center_row[None, None, :] - lowered).astype(jnp.int32).reshape(2, blocks * NEWL)


def levels(stream_key, shape, cuts, low, top_value):
    def one(axis_at, blocks):
        heights = jax.random.uniform(jax.random.fold_in(jax.random.fold_in(stream_key, 6), axis_at), (blocks,), jnp.float32, low / len(cuts), top_value / len(cuts))
        return jnp.repeat(jnp.exp(heights), shape[axis_at] // blocks).reshape((-1,) + (1,) * (len(shape) - axis_at - 1))

    loudness = one(*cuts[0])
    for cut in cuts[1:]:
        loudness = loudness * one(*cut)
    return loudness


def centred(key, dims, spread, bound, split=(), kind=jnp.bfloat16):
    drawn = jax.random.normal(key, dims, jnp.float32) * spread
    if len(split) > 0:
        drawn = levels(key, dims, split, -0.22, 0.18) * drawn
    return jnp.clip(drawn, min=-bound, max=bound).astype(kind)


def setup_inputs(seed: int = 0) -> dict:
    key_of = jax.random.split(jax.random.key(seed), 7)
    raw_pulses = centred(key_of[0], (PULSES, 2, NR), 1.0, 6.0, ((0, 32),))
    range_filter = centred(key_of[1], (2, NR), 0.7071, 4.0, (), jnp.float32)
    steer_angle = jnp.clip(jax.random.uniform(key_of[2], (NBT0, PULSES), jnp.float32, -3.140625, 3.140625), -3.140625, 3.140625)
    band_offsets = draw_band_offsets(jax.random.fold_in(key_of[6], 71), 0)
    band_weights = centred(key_of[4], (2, NEWL * N_BEAM * N_COMP, BAND), 0.25, 1.5, ((1, 8),), jnp.float32)
    beam_delay = jnp.clip(jax.random.uniform(key_of[5], (2, NEWL * N_BEAM * N_COMP), jnp.float32, -3.0, 3.0) * levels(key_of[5], (2, NEWL * N_BEAM * N_COMP), ((1, 8),), -0.4, 0.0), -3.0, 3.0)
    return dict(raw_pulses=raw_pulses, range_filter=range_filter, steer_angle=steer_angle, band_offsets=band_offsets, band_weights=band_weights, beam_delay=beam_delay)


def dft_table(length):
    index_row = jnp.arange(length, dtype=jnp.int32)
    product = (index_row[:, None] * index_row[None, :]) % length
    phase_angle = product.astype(jnp.float32) * (2.0 * math.pi / length)
    return jnp.cos(phase_angle).astype(jnp.bfloat16), (-jnp.sin(phase_angle)).astype(jnp.bfloat16)


def real_form(length):
    cos_part, sin_part = dft_table(length)
    upper_rows = jnp.concatenate([cos_part, sin_part], axis=1)
    lower_rows = jnp.concatenate([-sin_part, cos_part], axis=1)
    return jnp.concatenate([upper_rows, lower_rows], axis=0)


def twiddle():
    freq_index = jnp.arange(RADIX, dtype=jnp.int32)[:, None]
    time_index = jnp.arange(RADIX, dtype=jnp.int32)[None, :]
    phase_angle = ((freq_index * time_index) % NR).astype(jnp.float32) * (2.0 * math.pi / NR)
    return jnp.cos(phase_angle), -jnp.sin(phase_angle)


def compress(raw, range_filter):
    number = raw.shape[0]
    samples = raw.reshape(number, 2 * RADIX, RADIX).astype(jnp.float32)
    first_form = real_form(RADIX).astype(jnp.float32)
    section_one = jnp.einsum('pan,ak->pkn', samples, first_form, precision=lax.Precision.HIGHEST)
    cos_part, sin_part = twiddle()
    real_in = section_one[:, :RADIX]
    imag_in = section_one[:, RADIX:]
    turned = jnp.stack([real_in * cos_part - imag_in * sin_part, real_in * sin_part + imag_in * cos_part], 1)
    turned = turned.astype(jnp.bfloat16).astype(jnp.float32)
    second = real_form(RADIX).reshape(2, RADIX, 2, RADIX).astype(jnp.float32)
    spectrum = jnp.einsum('prkn,rnsm->psmk', turned, second, precision=lax.Precision.HIGHEST)
    spectrum = spectrum.reshape(number, 2, NR)
    factor = NR ** -0.5
    real_out = (spectrum[:, 0] * range_filter[0] - spectrum[:, 1] * range_filter[1]) * factor
    imag_out = (spectrum[:, 0] * range_filter[1] + spectrum[:, 1] * range_filter[0]) * factor
    return jnp.stack([real_out, imag_out], 1).astype(jnp.bfloat16)


def steering(phase_angle, factor):
    real_part = (jnp.cos(phase_angle) * factor).astype(jnp.bfloat16)
    imag_part = (jnp.sin(phase_angle) * factor).astype(jnp.bfloat16)
    return jnp.stack([jnp.stack([real_part, -imag_part], -1), jnp.stack([imag_part, real_part], -1)], 1)


def beam_term(weights, pulses):
    return jnp.einsum('kspq,pqr->ksr', weights.astype(jnp.float32), pulses.astype(jnp.float32),
                      precision=lax.Precision.HIGHEST)


def band_matrix(offset, weight, span):
    tap_index = offset[:, None] + BAND // 2 + jnp.arange(BAND, dtype=jnp.int32)[None, :]
    matches = tap_index[:, :, None] == jnp.arange(span, dtype=jnp.int32)[None, None, :]
    return jnp.sum(jnp.where(matches, weight[:, :, None], jnp.zeros_like(weight)[:, :, None]), axis=1)


def merge_level(subimage, level_index, band_offsets, band_weights, beam_delay):
    blocks = N_BEAM * N_COMP
    old_beams = NB0 * 2 ** level_index
    new_beams = 2 * old_beams
    column_base = NB0 * (2 ** (level_index + 1) - 2)
    margin = BAND // 2
    groups = subimage.shape[0] // 2
    padded = jnp.pad(subimage, ((0, 0), (margin, margin), (0, 0), (0, 0)))
    paired = padded.reshape(groups, 2, padded.shape[1], 2, NR)
    range_rows = jnp.arange(NR, dtype=jnp.int32).astype(jnp.float32)
    pieces = []
    for block in range(blocks):
        window = paired[:, :, block * old_beams: block * old_beams + old_beams + 2 * margin]
        col_start = block * NEWL + column_base
        real_sum = jnp.zeros((groups, new_beams, NR), jnp.float32)
        imag_sum = jnp.zeros((groups, new_beams, NR), jnp.float32)
        for parity in range(2):
            matrix = band_matrix(band_offsets[parity, col_start:col_start + new_beams],
                                 band_weights[parity, col_start:col_start + new_beams], old_beams + 2 * margin)
            blended = jnp.einsum('jw,gwsr->gjsr', matrix, window[:, parity], precision=lax.Precision.HIGHEST)
            phase_angle = beam_delay[parity, col_start:col_start + new_beams][:, None] * (1.0 + range_rows / NR)[None, :]
            cosine = jnp.cos(phase_angle)
            sine_part = jnp.sin(phase_angle)
            real_sum = real_sum + (cosine * blended[:, :, 0] - sine_part * blended[:, :, 1])
            imag_sum = imag_sum + (sine_part * blended[:, :, 0] + cosine * blended[:, :, 1])
        pieces.append(jnp.stack([real_sum, imag_sum], 2))
    return jnp.concatenate(pieces, 1)


def reference(raw_pulses, range_filter, steer_angle, band_offsets, band_weights, beam_delay):
    blocks = N_BEAM * N_COMP
    runs = raw_pulses.reshape(N_SUB, blocks, PDEV, 2, NR)
    angles = steer_angle.reshape(NBT0, N_SUB, blocks, PDEV).transpose(1, 2, 0, 3)
    factor = float(PSUB) ** -0.5

    def subaperture(sub_item):
        def add_run(summed, run_item):
            pulses = compress(run_item[0], range_filter)
            weights = steering(run_item[1], factor)
            return summed + beam_term(weights, pulses), None

        summed, _ = lax.scan(add_run, jnp.zeros((NBT0, 2, NR), jnp.float32), sub_item)
        return summed

    subimage = lax.map(subaperture, (runs, angles))
    for level_index in range(LEVELS):
        subimage = merge_level(subimage, level_index, band_offsets, band_weights, beam_delay)
    return subimage[0]
```

```python
import functools
import itertools
import math

import jax
import jax.numpy as jnp
import numpy as np
from jax import lax
from jax.experimental import pallas as pl
from jax.experimental.pallas import tpu as pltpu
from jax.sharding import PartitionSpec as P

BAND = 8
EXTRA = 8
FIELDS = 16
GROUP = 4
PIECES = 8
LAG = 3
LAG_TWO = 2
OUT_PIECES = 4
MESH = pl.DeviceIdType.MESH
F32 = jnp.float32
BF16 = jnp.bfloat16


def dft_table(length):
    index_row = np.arange(length, dtype=np.int32)
    product = index_row[:, None] * index_row[None, :] % length
    phase_angle = product.astype(np.float32) * np.float32(2.0 * math.pi / length)
    return np.cos(phase_angle).astype(BF16), (-np.sin(phase_angle)).astype(BF16)


def real_form(length):
    cos_part, sin_part = dft_table(length)
    upper_rows = np.concatenate([cos_part, sin_part], axis=1)
    lower_rows = np.concatenate([-sin_part, cos_part], axis=1)
    return np.concatenate([upper_rows, lower_rows], axis=0)


def twiddle(radix):
    index_row = np.arange(radix, dtype=np.int32)
    product = index_row[:, None] * index_row[None, :] % (radix * radix)
    phase_angle = product.astype(np.float32) * np.float32(2.0 * math.pi / (radix * radix))
    return np.stack([np.cos(phase_angle), -np.sin(phase_angle)], 0).astype(np.float32)


def split(value):
    high = value.astype(BF16)
    return high, (value - high.astype(F32)).astype(BF16)


def dot(a, b):
    return jnp.dot(a, b, preferred_element_type=F32)


class Plan:
    def __init__(self, counts, angle_shape, length, columns):
        self.sub, self.beam, self.comp = counts
        self.blocks = self.beam * self.comp
        self.beams, self.pulses = angle_shape
        self.first = self.beams // self.blocks
        self.length = length
        self.radix = math.isqrt(length)
        self.columns = columns
        self.group = min(GROUP, self.first)
        self.groups = self.first // self.group
        self.rows = 2 * self.group
        self.width = length // PIECES
        self.levels = self.sub.bit_length() - 1
        self.quarter = self.radix // self.sub
        self.share = self.quarter // self.comp
        self.outs = self.first * self.sub
        self.padded = -(-2 * columns // 128) * 128
        self.slots = self.comp + 2
        self.factor = float(self.pulses * self.blocks) ** (-0.5)
        self.sizes = []
        for level in range(self.levels):
            own = self.comp * self.first * 2 ** (level + 1)
            self.sizes.append(own + (0 if level == self.levels - 1 else 2 * EXTRA))
        self.depths = [2 * self.slots * self.first] + [2 * n for n in self.sizes[:-1]]
        near = {(0, d, e) for d in (-1, 0, 1) for e in range(self.comp)}
        near |= {(d, 0, e) for d in range(self.sub) for e in range(self.comp)}
        near |= {(0, d, 0) for d in range(self.beam)}
        self.peers = sorted({(d % self.sub, e % self.beam, f % self.comp) for d, e, f in near} - {(0, 0, 0)})
        self.table_peers = [
            (d, e)
            for d in (-1, 0, 1)
            for e in range(self.comp)
            if (d % self.beam, e) != (0, 0)
        ]
        self.swap_peers = [
            (d, e) for d in range(self.sub) for e in range(self.comp) if (d, e) != (0, 0)
        ]

    def pieces(self, level):
        new = self.first * 2 ** (level + 1)
        inner = [(k, 0, new) for k in range(self.comp)]
        if level == self.levels - 1:
            return inner
        return [(-1, new - EXTRA, EXTRA)] + inner + [(self.comp, 0, EXTRA)]


def fused_kernel(
    plan, angle_ref, raw_hbm, filter_hbm, table_ref, first_hbm, second_hbm, turn_hbm, out_ref,
    raw, weight, part, recv_one, held, recv_two, swap, first, second, turn, filt, blend, image,
    window, tables, fields, *rest,
):
    p = plan
    levels = p.levels
    lhs = rest[:levels]
    delay = rest[levels : 2 * levels]
    phase = rest[2 * levels : 3 * levels]
    (final, outbound, inbound, load_sem, const_sem, table_send, table_recv, one_send, one_recv,
     two_send, two_recv, swap_send, swap_recv, halo_send, halo_recv, out_send, out_recv) = rest[
        3 * levels :
    ]
    s = lax.axis_index("sub")
    b = lax.axis_index("beam")
    c = lax.axis_index("comp")
    has_low = b > 0
    has_high = b < p.beam - 1
    radix = p.radix

    def at(ds, db, dc):
        return {
            "sub": lax.rem(s + (ds % p.sub), p.sub),
            "beam": lax.rem(b + (db % p.beam), p.beam),
            "comp": lax.rem(c + (dc % p.comp), p.comp),
        }

    def remote(source, target, send, recv, place):
        return pltpu.make_async_remote_copy(
            src_ref=source, dst_ref=target, send_sem=send, recv_sem=recv, device_id=place,
            device_id_type=MESH,
        )

    loads = []
    for h in range(PIECES):
        cols = pl.ds(h * p.width, p.width)
        loads.append(
            pltpu.make_async_copy(raw_hbm.at[:, :, cols], raw.at[:, :, cols], load_sem.at[h])
        )
        loads[h].start()
    constants = [
        pltpu.make_async_copy(source, target, const_sem.at[i])
        for i, (source, target) in enumerate(
            [(first_hbm, first), (second_hbm, second), (turn_hbm, turn), (filter_hbm, filt)]
        )
    ]
    for copy in constants:
        copy.start()

    barrier = pltpu.get_barrier_semaphore()
    for place in p.peers:
        pl.semaphore_signal(barrier, inc=1, device_id=at(*place), device_id_type=MESH)

    angle = angle_ref[...]
    cos_part = (jnp.cos(angle) * p.factor).astype(BF16)
    sin_part = (jnp.sin(angle) * p.factor).astype(BF16)
    stacked = jnp.concatenate(
        [
            jnp.concatenate([cos_part, -sin_part], axis=1),
            jnp.concatenate([sin_part, cos_part], axis=1),
        ],
        axis=0,
    )
    count, deep = 2 * p.beams, 2 * p.pulses
    source = lax.broadcasted_iota(jnp.int32, (deep, deep), 0)
    target = lax.broadcasted_iota(jnp.int32, (deep, deep), 1)
    place = jnp.where(source < p.pulses, 2 * source, 2 * (source - p.pulses) + 1)
    spread = jnp.where(place == target, 1.0, 0.0).astype(BF16)
    target = lax.broadcasted_iota(jnp.int32, (count, count), 0)
    source = lax.broadcasted_iota(jnp.int32, (count, count), 1)

    def bits(value, size):
        return jnp.bitwise_and(value, size - 1), lax.shift_right_logical(
            value, jnp.full_like(value, size.bit_length() - 1)
        )

    within, upper = bits(target, p.group)
    half, upper = bits(upper, 2)
    beam_at, upper = bits(upper, p.beam)
    comp_at, group_at = bits(upper, p.comp)
    origin = half * p.beams + (
        (beam_at * p.comp + comp_at) * p.first + group_at * p.group + within
    )
    order = jnp.where(origin == source, 1.0, 0.0).astype(BF16)
    weight[...] = dot(order, dot(stacked, spread).astype(BF16)).astype(BF16)

    pl.semaphore_wait(barrier, len(p.peers))

    started = []
    table_copies = []

    def table_copy(i, db, dc):
        return remote(
            table_ref,
            tables.at[1 - db, lax.rem(c + p.comp, p.comp)],
            table_send.at[i], table_recv.at[i], at(0, db, dc),
        )

    for i, (db, dc) in enumerate(p.table_peers):
        copy = table_copy(i, db, dc)
        copy.start()
        table_copies.append(copy)

    def columns_of(h):
        return pl.ds(h * p.width, p.width)

    one, two, swaps = {}, {}, {}

    def form(h):
        loads[h].wait()
        pulses = raw[:, :, columns_of(h)].reshape(-1, p.width)
        product = dot(weight[...], pulses)
        part[:, :, :, :, columns_of(h)] = product.astype(BF16).reshape(
            p.groups, p.comp, p.beam, p.rows, p.width
        )

    def start_one(g, h):
        one[g, h] = []
        for d in range(1, p.comp):
            peer = lax.rem(c + d, p.comp)
            k = (g * PIECES + h) * (p.comp - 1) + d - 1
            copy = remote(
                part.at[g, peer, :, :, columns_of(h)],
                recv_one.at[d - 1, g, :, :, columns_of(h)],
                one_send.at[k], one_recv.at[k], at(0, 0, d),
            )
            copy.start()
            one[g, h].append(copy)

    def start_two(g, h):
        for copy in one[g, h]:
            copy.wait_recv()
        total = part[g, c, :, :, columns_of(h)].astype(F32)
        for d in range(1, p.comp):
            total += recv_one[d - 1, g, :, :, columns_of(h)].astype(F32)
        held[g, :, :, columns_of(h)] = total.astype(BF16)
        two[g, h] = []
        for d in range(1, p.beam):
            peer = lax.rem(b + d, p.beam)
            k = (g * PIECES + h) * (p.beam - 1) + d - 1
            copy = remote(
                held.at[g, peer, :, columns_of(h)],
                recv_two.at[d - 1, g, :, columns_of(h)],
                two_send.at[k], two_recv.at[k], at(0, d, 0),
            )
            copy.start()
            two[g, h].append(copy)

    def finish(g, h):
        for copy in two[g, h]:
            copy.wait_recv()
        total = part[g, c, b, :, columns_of(h)].astype(F32)
        for d in range(1, p.comp):
            total += recv_one[d - 1, g, b, :, columns_of(h)].astype(F32)
        for d in range(1, p.beam):
            total += recv_two[d - 1, g, :, columns_of(h)].astype(F32)
        for a in range(p.width // radix):
            swap[pl.ds(h * (p.width // radix) + a, p.rows, stride=radix), :] = total[
                :, a * radix : (a + 1) * radix
            ]

    def compress(g):
        factor = p.length ** (-0.5)
        h_real = filt[pl.ds(0, radix, stride=2), :] * factor
        h_imag = filt[pl.ds(1, radix, stride=2), :] * factor
        span = p.group * radix

        @pl.loop(0, p.group // 2)
        def _(pair):
            sides = []
            for u in range(2):
                row = pl.multiple_of((2 * pair + u) * radix, radix)
                sides.append(
                    jnp.concatenate(
                        [swap[pl.ds(row, radix), :], swap[pl.ds(row + span, radix), :]], axis=0
                    )
                )
            high, low = split(jnp.concatenate(sides, axis=1))
            section = dot(first[...], high) + dot(first[...], low)
            cos_turn, sin_turn = turn[0], turn[1]
            turned = []
            for u in range(2):
                real = section[:radix, u * radix : (u + 1) * radix]
                imag = section[radix:, u * radix : (u + 1) * radix]
                turned.append(
                    jnp.concatenate(
                        [
                            real * cos_turn - imag * sin_turn,
                            real * sin_turn + imag * cos_turn,
                        ],
                        axis=1,
                    )
                )
            high, low = split(jnp.concatenate(turned, axis=0))
            both_last = (((1,), (1,)), ((), ()))
            spectrum = lax.dot_general(second[...], high, both_last, preferred_element_type=F32)
            spectrum += lax.dot_general(second[...], low, both_last, preferred_element_type=F32)
            for u in range(2):
                real = spectrum[:radix, u * radix : (u + 1) * radix]
                imag = spectrum[radix:, u * radix : (u + 1) * radix]
                row = 2 * pair + u
                blend[pl.ds(row, radix, stride=p.rows), :] = real * h_real - imag * h_imag
                blend[pl.ds(row + p.group, radix, stride=p.rows), :] = (
                    real * h_imag + imag * h_real
                )

        image[g] = blend[...].reshape(radix, p.rows, radix).astype(BF16)
        swaps[g] = []
        for i, (ds, dc) in enumerate(p.swap_peers):
            where = at(ds, 0, dc)
            begin = (where["sub"] * p.comp + where["comp"]) * p.share
            k = g * len(p.swap_peers) + i
            copy = remote(
                image.at[g, pl.ds(begin, p.share)],
                window.at[s, 1 + c, g],
                swap_send.at[k], swap_recv.at[k], where,
            )
            copy.start()
            swaps[g].append(copy)
        window[s, 1 + c, g] = image[g, pl.ds((s * p.comp + c) * p.share, p.share)]

    def halo_copy(g, step):
        near, far = (1, p.comp + 1) if step < 0 else (p.comp, 0)
        k = 2 * g + (0 if step < 0 else 1)
        return remote(
            window.at[:, near, g], window.at[:, far, g], halo_send.at[k], halo_recv.at[k],
            {"beam": b + step},
        )

    def start_halo(g):
        for copy in swaps[g]:
            copy.wait_recv()

        @pl.when(has_low)
        def _():
            halo_copy(g, -1).start()

        @pl.when(has_high)
        def _():
            halo_copy(g, 1).start()

    def wait_halo(g):
        @pl.when(has_low)
        def _():
            halo_copy(g, 1).wait_recv()
            halo_copy(g, -1).wait_send()

        @pl.when(has_high)
        def _():
            halo_copy(g, -1).wait_recv()
            halo_copy(g, 1).wait_send()

    def read_tables():
        tables[1, c] = table_ref[...]
        for copy in table_copies:
            copy.wait_recv()
        for j in range(p.padded // 128):
            block = tables[:, :, :, j * 128 : (j + 1) * 128].reshape(-1, 128)
            short = 128 - block.shape[0]
            if short > 0:
                block = jnp.concatenate([block, jnp.zeros((short, 128), F32)], axis=0)
            fields[j * 128 : (j + 1) * 128, :] = block.T
        zeros = jnp.zeros(window.shape[:1] + window.shape[2:], BF16)

        @pl.when(jnp.logical_not(has_low))
        def _():
            window[:, 0] = zeros

        @pl.when(jnp.logical_not(has_high))
        def _():
            window[:, p.comp + 1] = zeros

    def fields_of(level, side):
        for step, begin, size in p.pieces(level):
            row = side * p.columns + p.first * (2 ** (level + 1) - 2) + begin
            device = (step + p.comp) if 0 <= step < p.comp else (p.comp - 1 if step < 0 else 2 * p.comp)
            yield step, size, row, device * FIELDS

    def build(level):
        depth, size = p.depths[level], p.sizes[level]
        child = p.first * 2**level
        lane = lax.broadcasted_iota(jnp.int32, (1, depth), 1)
        if level == 0:
            within, upper = bits(lane, p.group)
            half, upper = bits(upper, 2)
            group_at, slot = bits(upper, p.groups)
            beam_at = slot * p.first + group_at * p.group + within
        else:
            half = jnp.where(lane < depth // 2, 0, 1)
            beam_at = lane - half * (depth // 2)
        begin = p.first if level == 0 else EXTRA
        for side in range(2):
            done = 0
            for step, rows, row, base in fields_of(level, side):
                block = fields[row : row + rows, base : base + FIELDS]
                shift = block[:, BAND : BAND + 1].astype(jnp.int32)
                tap = beam_at - begin - step * child - shift
                band = jnp.zeros((rows, depth), F32)
                for t in range(BAND):
                    band += jnp.where(tap == t, block[:, t : t + 1], 0.0)
                if step < 0:
                    band = jnp.where(has_low, band, 0.0)
                if step >= p.comp:
                    band = jnp.where(has_high, band, 0.0)
                for r in range(2):
                    high, low = split(jnp.where(half == r, band, 0.0))
                    lhs[level][side, 0, r * size + done : r * size + done + rows, :] = high
                    lhs[level][side, 1, r * size + done : r * size + done + rows, :] = low
                delay[level][side, done : done + rows, :] = jnp.broadcast_to(
                    block[:, BAND + 1 : BAND + 2], (rows, radix)
                )
                done += rows

    def build_phases(begin, end):
        start = (s * p.comp + c) * p.share

        @pl.loop(begin, end)
        def _(m):
            for level in range(levels):
                for side in range(2):
                    factor = delay[level][side]
                    lane = lax.broadcasted_iota(jnp.int32, factor.shape, 1)
                    place = ((start + m) * radix + lane).astype(F32)
                    phase_angle = factor * (1.0 + place / p.length)
                    phase[level][0, side, m] = jnp.cos(phase_angle)
                    phase[level][1, side, m] = jnp.sin(phase_angle)

    def merge(m):
        def pair(load):
            return jnp.concatenate([load(m), load(m + 1)], axis=1)

        images = [
            pair(lambda k, i=i: window[i, :, :, k].reshape(p.depths[0], radix))
            for i in range(p.sub)
        ]
        for level in range(levels):
            size = p.sizes[level]
            merged = []
            for g in range(len(images) // 2):
                real, imag = 0.0, 0.0
                for side in range(2):
                    child = images[2 * g + side]
                    mixed = dot(lhs[level][side, 0], child) + dot(lhs[level][side, 1], child)
                    cosine = pair(lambda k: phase[level][0, side, k])
                    sine = pair(lambda k: phase[level][1, side, k])
                    real += cosine * mixed[:size] - sine * mixed[size:]
                    imag += sine * mixed[:size] + cosine * mixed[size:]
                merged.append((real, imag))
            if level + 1 < levels:
                images = [jnp.concatenate(parts, axis=0).astype(BF16) for parts in merged]
        for r in range(2):
            for k in range(p.comp):
                for u in range(2):
                    value = merged[0][r][k * p.outs : (k + 1) * p.outs, u * radix : (u + 1) * radix]
                    final[k, m + u, r * p.outs : (r + 1) * p.outs, :] = value
                    outbound[k, m + u, r * p.outs : (r + 1) * p.outs, :] = value.astype(BF16)

    def place_out(source, m, column):
        for r in range(2):
            value = source[r * p.outs : (r + 1) * p.outs].astype(F32)
            out_ref[pl.ds(2 * (column * p.share + m) + r, p.outs, stride=2 * p.quarter), :] = value

    units = [(g, h) for g in range(p.groups) for h in range(PIECES)]
    total_units = len(units)
    per_step = -(-p.share // PIECES)
    pending = []
    for u in range(total_units + LAG + LAG_TWO):
        if u < PIECES:
            form(u)
        if u < total_units:
            start_one(*units[u])
        if 0 <= u - LAG < total_units:
            start_two(*units[u - LAG])
        v = u - LAG - LAG_TWO
        if pending and v >= pending[0][0]:
            start_halo(pending.pop(0)[1])
        if u == PIECES:
            read_tables()
            for copy in constants:
                copy.wait()
            for level in range(levels):
                build(level)
        if PIECES <= u < 2 * PIECES:
            begin = min((u - PIECES) * per_step, p.share)
            end = min(begin + per_step, p.share)
            if end > begin:
                build_phases(begin, end)
        if v >= 0:
            finish(*units[v])
            g, h = units[v]
            if h == PIECES - 1:
                compress(g)
                pending.append((v + 2, g))
    for _, g in pending:
        start_halo(g)
    for g in range(p.groups):
        wait_halo(g)

    chunk = p.share // OUT_PIECES
    outs = []
    for o in range(OUT_PIECES):
        @pl.loop(0, chunk // 2)
        def _(i, o=o):
            merge(o * chunk + 2 * i)

        for d in range(1, p.comp):
            peer = lax.rem(c + d, p.comp)
            k = (d - 1) * OUT_PIECES + o
            copy = remote(
                outbound.at[peer, pl.ds(o * chunk, chunk)],
                inbound.at[d - 1, pl.ds(o * chunk, chunk)],
                out_send.at[k], out_recv.at[k], at(0, 0, d),
            )
            copy.start()
            outs.append((o, d, copy))

    @pl.loop(0, p.share)
    def _(m):
        place_out(final[c, m], m, c)

    for o, d, copy in outs:
        copy.wait_recv()
        origin = lax.rem(c + p.comp - d, p.comp)

        @pl.loop(0, chunk)
        def _(i, o=o, d=d, origin=origin):
            place_out(inbound[d - 1, o * chunk + i], o * chunk + i, origin)

    for copy in itertools.chain(
        table_copies, *one.values(), *two.values(), *swaps.values(), (entry[2] for entry in outs)
    ):
        copy.wait_send()


def fused(plan, angle, raw, filt, table):
    p = plan
    constants = real_form(p.radix)
    any_space = pl.BlockSpec(memory_space=pl.ANY)
    vmem = pl.BlockSpec(memory_space=pltpu.VMEM)
    dma = pltpu.SemaphoreType.DMA
    radix = p.radix
    units = p.groups * PIECES
    return pl.pallas_call(
        functools.partial(fused_kernel, p),
        out_shape=jax.ShapeDtypeStruct((p.outs * 2 * p.quarter, radix), F32),
        in_specs=[vmem, any_space, any_space, vmem, any_space, any_space, any_space],
        out_specs=vmem,
        scratch_shapes=[
            pltpu.VMEM(raw.shape, BF16),
            pltpu.VMEM((2 * p.beams, 2 * p.pulses), BF16),
            pltpu.VMEM((p.groups, p.comp, p.beam, p.rows, p.length), BF16),
            pltpu.VMEM((p.comp - 1, p.groups, p.beam, p.rows, p.length), BF16),
            pltpu.VMEM((p.groups, p.beam, p.rows, p.length), BF16),
            pltpu.VMEM((p.beam - 1, p.groups, p.rows, p.length), BF16),
            pltpu.VMEM((p.rows * radix, radix), F32),
            pltpu.VMEM((2 * radix, 2 * radix), BF16),
            pltpu.VMEM((2 * radix, 2 * radix), BF16),
            pltpu.VMEM((2, radix, radix), F32),
            pltpu.VMEM((2 * radix, radix), F32),
            pltpu.VMEM((p.rows * radix, radix), F32),
            pltpu.VMEM((p.groups, radix, p.rows, radix), BF16),
            pltpu.VMEM((p.sub, p.slots, p.groups, p.share, p.rows, radix), BF16),
            pltpu.VMEM((3, p.comp, FIELDS, p.padded), F32),
            pltpu.VMEM((p.padded, 128), F32),
            *[pltpu.VMEM((2, 2, 2 * n, k), BF16) for n, k in zip(p.sizes, p.depths)],
            *[pltpu.VMEM((2, n, radix), F32) for n in p.sizes],
            *[pltpu.VMEM((2, 2, p.share, n, radix), F32) for n in p.sizes],
            pltpu.VMEM((p.comp, p.share, 2 * p.outs, radix), F32),
            pltpu.VMEM((p.comp, p.share, 2 * p.outs, radix), BF16),
            pltpu.VMEM((p.comp - 1, p.share, 2 * p.outs, radix), BF16),
            dma((PIECES,)),
            dma((4,)),
            dma((len(p.table_peers),)),
            dma((len(p.table_peers),)),
            dma((units * (p.comp - 1),)),
            dma((units * (p.comp - 1),)),
            dma((units * (p.beam - 1),)),
            dma((units * (p.beam - 1),)),
            dma((p.groups * len(p.swap_peers),)),
            dma((p.groups * len(p.swap_peers),)),
            dma((2 * p.groups,)),
            dma((2 * p.groups,)),
            dma(((p.comp - 1) * OUT_PIECES,)),
            dma(((p.comp - 1) * OUT_PIECES,)),
        ],
        compiler_params=pltpu.CompilerParams(
            collective_id=0, has_side_effects=True, vmem_limit_bytes=58 * 2**20
        ),
    )(
        angle, raw, filt, table, jnp.asarray(constants.T), jnp.asarray(constants.T),
        jnp.asarray(twiddle(radix)),
    )


def body(raw_pulses, range_filter, steer_angle, band_offsets, band_weights, beam_delay):
    counts = (lax.axis_size("sub"), lax.axis_size("beam"), lax.axis_size("comp"))
    columns = band_offsets.shape[1]
    plan = Plan(counts, steer_angle.shape, raw_pulses.shape[2], columns)
    radix = plan.radix
    table = jnp.concatenate(
        [
            band_weights.transpose(2, 0, 1).reshape(BAND, 2 * columns),
            band_offsets.astype(F32).reshape(1, 2 * columns),
            beam_delay.reshape(1, 2 * columns),
        ],
        axis=0,
    )
    table = jnp.pad(
        table, ((0, FIELDS - table.shape[0]), (0, plan.padded - 2 * columns))
    )
    filt = range_filter.reshape(2, radix, radix).transpose(1, 0, 2).reshape(2 * radix, radix)
    out = fused(plan, steer_angle, raw_pulses, filt, table)
    out = out.reshape(plan.outs, plan.quarter, 2, radix).transpose(0, 2, 1, 3)
    return out.reshape(plan.outs, 2, plan.quarter * radix)


def solution(mesh):
    in_specs = (
        P(("sub", "beam", "comp"), None, None),
        P(),
        P(None, ("sub", "beam", "comp")),
        P(None, ("beam", "comp")),
        P(None, ("beam", "comp"), None),
        P(None, ("beam", "comp")),
    )
    out_specs = P(("beam", "comp"), None, "sub")
    return jax.shard_map(body, mesh=mesh, in_specs=in_specs, out_specs=out_specs, check_vma=False)
```

```python
import functools
import itertools
import math

import jax
import jax.numpy as jnp
import numpy as np
from jax import lax
from jax.experimental import pallas as pl
from jax.experimental.pallas import tpu as pltpu
from jax.sharding import PartitionSpec as P

BAND = 8
EXTRA = 8
SIDE = 12
GROUP = 2
PIECES = 8
LAG = 4
LAG_TWO = 3
OUT_PIECES = 4
HALO_LAG = 4
LIMIT = 54 * 2**20
STORES = 4
MESH = pl.DeviceIdType.MESH
F32 = jnp.float32
BF16 = jnp.bfloat16


def dft_table(length):
    index_row = np.arange(length, dtype=np.int32)
    product = index_row[:, None] * index_row[None, :] % length
    phase_angle = product.astype(np.float32) * np.float32(2.0 * math.pi / length)
    return np.cos(phase_angle).astype(BF16), (-np.sin(phase_angle)).astype(BF16)


def real_form(length):
    cos_part, sin_part = dft_table(length)
    upper_rows = np.concatenate([cos_part, sin_part], axis=1)
    lower_rows = np.concatenate([-sin_part, cos_part], axis=1)
    return np.concatenate([upper_rows, lower_rows], axis=0)


def twiddle(radix):
    index_row = np.arange(radix, dtype=np.int32)
    product = index_row[:, None] * index_row[None, :] % (radix * radix)
    phase_angle = product.astype(np.float32) * np.float32(2.0 * math.pi / (radix * radix))
    return np.stack([np.cos(phase_angle), -np.sin(phase_angle)], 0).astype(np.float32)


def split(value):
    high = value.astype(BF16)
    return high, (value - high.astype(F32)).astype(BF16)


def dot(a, b):
    return jnp.dot(a, b, preferred_element_type=F32)


class Plan:
    def __init__(self, counts, angle_shape, length, columns):
        self.sub, self.beam, self.comp = counts
        self.blocks = self.beam * self.comp
        self.beams, self.pulses = angle_shape
        self.first = self.beams // self.blocks
        self.length = length
        self.radix = math.isqrt(length)
        self.columns = columns
        self.group = min(GROUP, self.first)
        self.groups = self.first // self.group
        self.rows = 2 * self.group
        self.width = length // PIECES
        self.levels = self.sub.bit_length() - 1
        self.quarter = self.radix // self.sub
        self.share = self.quarter // self.comp
        self.outs = self.first * self.sub
        self.padded = -(-columns // 128) * 128
        self.stages = self.beam.bit_length() - 1
        self.slots = self.comp + 2
        self.factor = float(self.pulses * self.blocks) ** (-0.5)
        self.sizes = []
        for level in range(self.levels):
            own = self.comp * self.first * 2 ** (level + 1)
            self.sizes.append(own + (0 if level == self.levels - 1 else 2 * EXTRA))
        self.depths = [2 * self.slots * self.first] + [2 * n for n in self.sizes[:-1]]
        near = {(0, d, e) for d in (-1, 0, 1) for e in range(self.comp)}
        near |= {(d, 0, e) for d in range(self.sub) for e in range(self.comp)}
        near |= {(0, d, 0) for d in range(self.beam)}
        self.peers = sorted({(d % self.sub, e % self.beam, f % self.comp) for d, e, f in near} - {(0, 0, 0)})
        need = BAND // 2
        for _ in range(self.levels - 1):
            need = (need + 1) // 2 + BAND // 2
        need = min(need, self.first) if self.comp > 1 else self.first
        self.edges = [g for g in range(self.groups) if g * self.group < need]
        self.swap_peers = [
            (d, e) for d in range(self.sub) for e in range(self.comp) if (d, e) != (0, 0)
        ]

    def pieces(self, level):
        new = self.first * 2 ** (level + 1)
        inner = [(k, 0, new) for k in range(self.comp)]
        if level == self.levels - 1:
            return inner
        return [(-1, new - EXTRA, EXTRA)] + inner + [(self.comp, 0, EXTRA)]


def fused_kernel(
    plan, angle_hbm, raw_hbm, filter_hbm, weights_hbm, offsets_hbm, delay_hbm, first_hbm,
    second_hbm, turn_hbm, out_ref, angle_ref, weights_ref, offsets_ref, delay_ref, raw, weight, part, recv_one, swap, first, second, turn, filt,
    blend, image, window, mine, tables, fields, *rest,
):
    p = plan
    levels = p.levels
    rest = list(rest)

    def take(number):
        taken = rest[:number]
        del rest[:number]
        return taken

    held, recv_two = take(p.stages), take(p.stages)
    lhs, delay, phase = take(levels), take(levels), take(levels)
    (final, outbound, inbound, load_sem, const_sem, table_send, table_recv, one_send, one_recv,
     two_send, two_recv, swap_send, swap_recv, halo_send, halo_recv, out_send, out_recv) = rest
    s = lax.axis_index("sub")
    b = lax.axis_index("beam")
    c = lax.axis_index("comp")
    has_low = b > 0
    has_high = b < p.beam - 1
    radix = p.radix

    def at(ds, db, dc):
        return {
            "sub": lax.rem(s + (ds % p.sub), p.sub),
            "beam": lax.rem(b + (db % p.beam), p.beam),
            "comp": lax.rem(c + (dc % p.comp), p.comp),
        }

    def remote(source, target, send, recv, place):
        return pltpu.make_async_remote_copy(
            src_ref=source, dst_ref=target, send_sem=send, recv_sem=recv, device_id=place,
            device_id_type=MESH,
        )

    angle_load = pltpu.make_async_copy(angle_hbm, angle_ref, const_sem.at[7])
    angle_load.start()
    loads = []
    for h in range(PIECES):
        cols = pl.ds(h * p.width, p.width)
        loads.append(
            pltpu.make_async_copy(raw_hbm.at[:, :, cols], raw.at[:, :, cols], load_sem.at[h])
        )
        loads[h].start()
    constants = [
        pltpu.make_async_copy(source, target, const_sem.at[i])
        for i, (source, target) in enumerate(
            [
                (weights_hbm, weights_ref), (offsets_hbm, offsets_ref), (delay_hbm, delay_ref),
                (first_hbm, first), (second_hbm, second), (turn_hbm, turn), (filter_hbm, filt),
            ]
        )
    ]
    for copy in constants:
        copy.start()

    window[:, 0] = jnp.zeros(window.shape[:1] + window.shape[2:], BF16)
    window[:, p.comp + 1] = jnp.zeros(window.shape[:1] + window.shape[2:], BF16)
    barrier = pltpu.get_barrier_semaphore()
    for place in p.peers:
        pl.semaphore_signal(barrier, inc=1, device_id=at(*place), device_id_type=MESH)

    angle_load.wait()
    angle = angle_ref[...]
    cos_part = (jnp.cos(angle) * p.factor).astype(BF16)
    sin_part = (jnp.sin(angle) * p.factor).astype(BF16)
    stacked = jnp.concatenate(
        [
            jnp.concatenate([cos_part, -sin_part], axis=1),
            jnp.concatenate([sin_part, cos_part], axis=1),
        ],
        axis=0,
    )
    count, deep = 2 * p.beams, 2 * p.pulses
    source = lax.broadcasted_iota(jnp.int32, (deep, deep), 0)
    target = lax.broadcasted_iota(jnp.int32, (deep, deep), 1)
    place = jnp.where(source < p.pulses, 2 * source, 2 * (source - p.pulses) + 1)
    spread = jnp.where(place == target, 1.0, 0.0).astype(BF16)
    target = lax.broadcasted_iota(jnp.int32, (count, count), 0)
    source = lax.broadcasted_iota(jnp.int32, (count, count), 1)

    def bits(value, size):
        return jnp.bitwise_and(value, size - 1), lax.shift_right_logical(
            value, jnp.full_like(value, size.bit_length() - 1)
        )

    def order_of(group_at, comp_at):
        return jnp.where(comp_at == p.comp - 1, p.groups - 1 - group_at, group_at)

    within, upper = bits(target, p.group)
    half, upper = bits(upper, 2)
    beam_at, upper = bits(upper, p.beam)
    comp_at, group_at = bits(upper, p.comp)
    group_at = order_of(group_at, comp_at)
    origin = half * p.beams + (
        (beam_at * p.comp + comp_at) * p.first + group_at * p.group + within
    )
    order = jnp.where(origin == source, 1.0, 0.0).astype(BF16)
    weight[...] = dot(order, dot(stacked, spread).astype(BF16)).astype(BF16)

    pl.semaphore_wait(barrier, len(p.peers))

    for copy in constants[:3]:
        copy.wait()
    mine[...] = jnp.zeros(mine.shape, F32)
    for side in range(2):
        row = side * SIDE
        mine[row : row + BAND, : p.columns] = weights_ref[side]
        mine[row + BAND : row + BAND + 1, : p.columns] = offsets_ref[side : side + 1].astype(F32)
        mine[row + BAND + 1 : row + BAND + 2, : p.columns] = delay_ref[side : side + 1]
    tables[1 + c] = mine[...]

    def table_copy(db, dc):
        slot = 1 + c if db == 0 else (0 if db > 0 else p.comp + 1)
        k = (db + 1) * p.comp + dc
        r = dc if db == 0 else (0 if db > 0 else p.comp)
        return remote(mine, tables.at[slot], table_send.at[k], table_recv.at[r], at(0, db, dc))

    def table_ends(action):
        @pl.when(c == p.comp - 1)
        def _():
            for e in range(p.comp):
                action(table_copy(1, e))

        @pl.when(c == 0)
        def _():
            for e in range(p.comp):
                action(table_copy(-1, e))

    for e in range(1, p.comp):
        table_copy(0, e).start()
    table_ends(lambda copy: copy.start())

    def columns_of(h):
        return pl.ds(h * p.width, p.width)

    one, two, swaps = {}, {}, {}

    def bit(stage):
        return lax.rem(lax.div(b, 2**stage), 2)

    def form(h):
        loads[h].wait()
        pulses = raw[:, :, columns_of(h)].reshape(-1, p.width)
        product = dot(weight[...], pulses)
        part[:, :, :, :, columns_of(h)] = product.astype(BF16).reshape(
            p.groups, p.comp, p.beam, p.rows, p.width
        )

    def start_one(g, h):
        one[g, h] = []
        for d in range(1, p.comp):
            peer = lax.rem(c + d, p.comp)
            k = (g * PIECES + h) * (p.comp - 1) + d - 1
            copy = remote(
                part.at[g, peer, :, :, columns_of(h)],
                recv_one.at[d - 1, g, :, :, columns_of(h)],
                one_send.at[k], one_recv.at[k], at(0, 0, d),
            )
            copy.start()
            one[g, h].append(copy)

    def send_two(stage, g, h, total):
        held[stage][g, :, :, :, columns_of(h)] = total.astype(BF16).reshape(
            -1, 2, p.rows, p.width
        )
        k = (g * PIECES + h) * p.stages + stage
        copy = remote(
            held[stage].at[g, :, 1 - bit(stage), :, columns_of(h)],
            recv_two[stage].at[g, :, :, columns_of(h)],
            two_send.at[k], two_recv.at[k],
            {"beam": b + (1 - 2 * bit(stage)) * 2**stage},
        )
        copy.start()
        two[stage, g, h] = copy

    def start_two(g, h):
        for copy in one[g, h]:
            copy.wait_recv()
        total = part[g, c, :, :, columns_of(h)].astype(F32)
        for d in range(1, p.comp):
            total += recv_one[d - 1, g, :, :, columns_of(h)].astype(F32)
        send_two(0, g, h, total)

    def gathered(stage, g, h):
        two[stage, g, h].wait_recv()
        total = held[stage][g, :, bit(stage), :, columns_of(h)].astype(F32)
        return total + recv_two[stage][g, :, :, columns_of(h)].astype(F32)

    def finish(g, h):
        total = gathered(p.stages - 1, g, h)[0]
        for a in range(p.width // radix):
            swap[pl.ds(h * (p.width // radix) + a, p.rows, stride=radix), :] = total[
                :, a * radix : (a + 1) * radix
            ]

    deferred = []

    def compress(g, deferring):
        factor = p.length ** (-0.5)
        h_real = filt[pl.ds(0, radix, stride=2), :] * factor
        h_imag = filt[pl.ds(1, radix, stride=2), :] * factor
        span = p.group * radix

        @pl.loop(0, p.group // 2)
        def _(pair):
            sides = []
            for u in range(2):
                row = pl.multiple_of((2 * pair + u) * radix, radix)
                sides.append(
                    jnp.concatenate(
                        [swap[pl.ds(row, radix), :], swap[pl.ds(row + span, radix), :]], axis=0
                    )
                )
            high, low = split(jnp.concatenate(sides, axis=1))
            section = dot(first[...], high) + dot(first[...], low)
            cos_turn, sin_turn = turn[0], turn[1]
            turned = []
            for u in range(2):
                real = section[:radix, u * radix : (u + 1) * radix]
                imag = section[radix:, u * radix : (u + 1) * radix]
                turned.append(
                    jnp.concatenate(
                        [
                            real * cos_turn - imag * sin_turn,
                            real * sin_turn + imag * cos_turn,
                        ],
                        axis=1,
                    )
                )
            high, low = split(jnp.concatenate(turned, axis=0))
            both_last = (((1,), (1,)), ((), ()))
            spectrum = lax.dot_general(second[...], high, both_last, preferred_element_type=F32)
            spectrum += lax.dot_general(second[...], low, both_last, preferred_element_type=F32)
            for u in range(2):
                real = spectrum[:radix, u * radix : (u + 1) * radix]
                imag = spectrum[radix:, u * radix : (u + 1) * radix]
                row = 2 * pair + u
                blend[pl.ds(row, radix, stride=p.rows), :] = real * h_real - imag * h_imag
                blend[pl.ds(row + p.group, radix, stride=p.rows), :] = (
                    real * h_imag + imag * h_real
                )

        image[g] = blend[...].reshape(radix, p.rows, radix).astype(BF16)
        window[s, 1 + c, g] = image[g, pl.ds((s * p.comp + c) * p.share, p.share)]
        number = OUT_PIECES if g == p.groups - 1 else 1
        size = p.share // number
        for o in range(number):
            swaps[g, o] = []
            for i, (ds, dc) in enumerate(p.swap_peers):
                where = at(ds, 0, dc)
                begin = (where["sub"] * p.comp + where["comp"]) * p.share + o * size
                k = (g + o) * len(p.swap_peers) + i
                copy = remote(
                    image.at[g, pl.ds(begin, size)],
                    window.at[s, 1 + c, g, pl.ds(o * size, size)],
                    swap_send.at[k], swap_recv.at[k], where,
                )
                swaps[g, o].append(copy)
                if dc == 0 or not deferring:
                    copy.start()
                else:
                    deferred.append(copy)

    def halo_copy(g, o, step):
        near, far = (1, p.comp + 1) if step < 0 else (p.comp, 0)
        size = p.share // (OUT_PIECES if g == p.groups - 1 else 1)
        k = 2 * (g + o) + (0 if step < 0 else 1)
        return remote(
            window.at[:, near, g, pl.ds(o * size, size)],
            window.at[:, far, g, pl.ds(o * size, size)],
            halo_send.at[k], halo_recv.at[k], {"beam": b + step},
        )

    def start_halo(g, o=0):
        for copy in swaps[g, o]:
            copy.wait_recv()
        if g not in p.edges:
            return

        @pl.when(has_low)
        def _():
            halo_copy(g, o, -1).start()

        @pl.when(has_high)
        def _():
            halo_copy(g, o, 1).start()

    def wait_halo(g, o=0):
        if g not in p.edges:
            return

        @pl.when(has_low)
        def _():
            halo_copy(g, o, 1).wait_recv()
            halo_copy(g, o, -1).wait_send()

        @pl.when(has_high)
        def _():
            halo_copy(g, o, -1).wait_recv()
            halo_copy(g, o, 1).wait_send()

    def read_tables():
        for e in range(1, p.comp):
            table_copy(0, e).wait_recv()
        table_copy(1, 0).wait_recv()
        table_copy(-1, 0).wait_recv()
        for j in range(p.padded // 128):
            block = tables[:, :, j * 128 : (j + 1) * 128].reshape(-1, 128)
            short = 128 - block.shape[0]
            if short > 0:
                block = jnp.concatenate([block, jnp.zeros((short, 128), F32)], axis=0)
            fields[j * 128 : (j + 1) * 128, :] = block.T

    def fields_of(level, side):
        for step, begin, size in p.pieces(level):
            row = p.first * (2 ** (level + 1) - 2) + begin
            yield step, size, row, (step + 1) * 2 * SIDE + side * SIDE

    def build(level):
        depth, size = p.depths[level], p.sizes[level]
        child = p.first * 2**level
        lane = lax.broadcasted_iota(jnp.int32, (1, depth), 1)
        if level == 0:
            within, upper = bits(lane, p.group)
            half, upper = bits(upper, 2)
            group_at, slot = bits(upper, p.groups)
            comp_at = jnp.where(slot == 0, p.comp - 1, jnp.where(slot > p.comp, 0, slot - 1))
            group_at = order_of(group_at, comp_at)
            beam_at = slot * p.first + group_at * p.group + within
        else:
            half = jnp.where(lane < depth // 2, 0, 1)
            beam_at = lane - half * (depth // 2)
        begin = p.first if level == 0 else EXTRA
        for side in range(2):
            done = 0
            for step, rows, row, base in fields_of(level, side):
                block = fields[row : row + rows, base : base + SIDE]
                shift = block[:, BAND : BAND + 1].astype(jnp.int32)
                tap = beam_at - begin - step * child - shift
                band = jnp.zeros((rows, depth), F32)
                for t in range(BAND):
                    band += jnp.where(tap == t, block[:, t : t + 1], 0.0)
                if step < 0:
                    band = jnp.where(has_low, band, 0.0)
                if step >= p.comp:
                    band = jnp.where(has_high, band, 0.0)
                for r in range(2):
                    high, low = split(jnp.where(half == r, band, 0.0))
                    lhs[level][side, 0, r * size + done : r * size + done + rows, :] = high
                    lhs[level][side, 1, r * size + done : r * size + done + rows, :] = low
                delay[level][side, done : done + rows, :] = jnp.broadcast_to(
                    block[:, BAND + 1 : BAND + 2], (rows, radix)
                )
                done += rows

    def build_phases(begin, end):
        start = (s * p.comp + c) * p.share

        @pl.loop(begin, end)
        def _(m):
            for level in range(levels):
                for side in range(2):
                    factor = delay[level][side]
                    lane = lax.broadcasted_iota(jnp.int32, factor.shape, 1)
                    place = ((start + m) * radix + lane).astype(F32)
                    phase_angle = factor * (1.0 + place / p.length)
                    phase[level][0, side, m] = jnp.cos(phase_angle)
                    phase[level][1, side, m] = jnp.sin(phase_angle)

    def merge(m):
        def pair(load):
            return jnp.concatenate([load(m), load(m + 1)], axis=1)

        images = [
            pair(lambda k, i=i: window[i, :, :, k].reshape(p.depths[0], radix))
            for i in range(p.sub)
        ]
        for level in range(levels):
            size = p.sizes[level]
            merged = []
            for g in range(len(images) // 2):
                real, imag = 0.0, 0.0
                for side in range(2):
                    child = images[2 * g + side]
                    mixed = dot(lhs[level][side, 0], child) + dot(lhs[level][side, 1], child)
                    cosine = pair(lambda k: phase[level][0, side, k])
                    sine = pair(lambda k: phase[level][1, side, k])
                    real += cosine * mixed[:size] - sine * mixed[size:]
                    imag += sine * mixed[:size] + cosine * mixed[size:]
                merged.append((real, imag))
            if level + 1 < levels:
                images = [jnp.concatenate(parts, axis=0).astype(BF16) for parts in merged]
        for r in range(2):
            for k in range(p.comp):
                for u in range(2):
                    value = merged[0][r][k * p.outs : (k + 1) * p.outs, u * radix : (u + 1) * radix]
                    final[k, m + u, r * p.outs : (r + 1) * p.outs, :] = value
                    outbound[k, m + u, r * p.outs : (r + 1) * p.outs, :] = value.astype(BF16)

    def place_out(source, m, column):
        for r in range(2):
            value = source[r * p.outs : (r + 1) * p.outs].astype(F32)
            out_ref[pl.ds(2 * (column * p.share + m) + r, p.outs, stride=2 * p.quarter), :] = value

    units = [(g, h) for g in range(p.groups) for h in range(PIECES)]
    total_units = len(units)
    idle = range(PIECES, 2 * PIECES)
    per_step = -(-p.share // len(idle))
    pending = []
    last = p.groups - 1
    drain = LAG + LAG_TWO * p.stages
    for u in range(total_units + drain):
        if u < PIECES:
            form(u)
        if u < total_units:
            start_one(*units[u])
        if u == total_units - 1:
            for copy in deferred:
                copy.start()
        if 0 <= u - LAG < total_units:
            start_two(*units[u - LAG])
        for stage in range(1, p.stages):
            v = u - LAG - LAG_TWO * stage
            if 0 <= v < total_units:
                send_two(stage, *units[v], gathered(stage - 1, *units[v]))
        v = u - drain
        while pending and v >= pending[0][0]:
            start_halo(pending.pop(0)[1])
        if u == PIECES:
            read_tables()
            for copy in constants[3:]:
                copy.wait()
            for level in range(levels):
                build(level)
        if u in idle:
            begin = min((u - PIECES) * per_step, p.share)
            end = min(begin + per_step, p.share)
            if end > begin:
                build_phases(begin, end)
        if v >= 0:
            finish(*units[v])
            g, h = units[v]
            if h == PIECES - 1:
                compress(g, u < total_units)
                if g < last:
                    pending.append((max(v + HALO_LAG, total_units - drain + 4), g))
    for _, g in pending:
        start_halo(g)
    for g in range(last):
        wait_halo(g)

    chunk = p.share // OUT_PIECES
    outs = []

    def merge_piece(o):
        @pl.loop(0, chunk // 2)
        def _(i):
            merge(o * chunk + 2 * i)

        for d in range(1, p.comp):
            peer = lax.rem(c + d, p.comp)
            k = (d - 1) * OUT_PIECES + o
            copy = remote(
                outbound.at[peer, pl.ds(o * chunk, chunk)],
                inbound.at[d - 1, pl.ds(o * chunk, chunk)],
                out_send.at[k], out_recv.at[k], at(0, 0, d),
            )
            copy.start()
            outs.append((o, d, copy))

    for o in range(OUT_PIECES):
        start_halo(last, o)
        if last not in p.edges:
            merge_piece(o)
    if last in p.edges:
        for o in range(OUT_PIECES):
            wait_halo(last, o)
            merge_piece(o)

    @pl.loop(0, p.share)
    def _(m):
        place_out(final[c, m], m, c)

    for o, d, copy in outs:
        copy.wait_recv()
        origin = lax.rem(c + p.comp - d, p.comp)

        @pl.loop(0, chunk)
        def _(i, o=o, d=d, origin=origin):
            place_out(inbound[d - 1, o * chunk + i], o * chunk + i, origin)

    for e in range(1, p.comp):
        table_copy(0, e).wait_send()
    table_ends(lambda copy: copy.wait_send())
    for copy in itertools.chain(
        *one.values(), two.values(), *swaps.values(), (entry[2] for entry in outs)
    ):
        copy.wait_send()


def store_kernel(value_ref, out_hbm, sem):
    size = value_ref.shape[0] // STORES
    copies = [
        pltpu.make_async_copy(
            value_ref.at[pl.ds(i * size, size)], out_hbm.at[pl.ds(i * size, size)], sem.at[i]
        )
        for i in range(STORES)
    ]
    for copy in copies:
        copy.start()
    for copy in copies:
        copy.wait()


def store(value):
    return pl.pallas_call(
        store_kernel,
        out_shape=jax.ShapeDtypeStruct(value.shape, value.dtype),
        in_specs=[pl.BlockSpec(memory_space=pltpu.VMEM)],
        out_specs=pl.BlockSpec(memory_space=pl.ANY),
        scratch_shapes=[pltpu.SemaphoreType.DMA((STORES,))],
        compiler_params=pltpu.CompilerParams(vmem_limit_bytes=8 * 2**20),
    )(value)


def fused(plan, angle, raw, filt, weights, offsets, delay):
    p = plan
    constants = real_form(p.radix)
    dma = pltpu.SemaphoreType.DMA
    radix = p.radix
    units = p.groups * PIECES
    halves = [p.beam // 2 ** (t + 1) for t in range(p.stages)]
    swap_count = p.groups - 1 + OUT_PIECES
    return pl.pallas_call(
        functools.partial(fused_kernel, p),
        out_shape=pltpu.VMEM((p.outs * 2 * p.quarter, radix), F32),
        in_specs=[pl.BlockSpec(memory_space=pltpu.HBM)] * 9,
        out_specs=pl.BlockSpec(memory_space=pltpu.VMEM),
        scratch_shapes=[
            pltpu.VMEM(angle.shape, F32),
            pltpu.VMEM(weights.shape, F32),
            pltpu.VMEM(offsets.shape, jnp.int32),
            pltpu.VMEM(delay.shape, F32),
            pltpu.VMEM(raw.shape, BF16),
            pltpu.VMEM((2 * p.beams, 2 * p.pulses), BF16),
            pltpu.VMEM((p.groups, p.comp, p.beam, p.rows, p.length), BF16),
            pltpu.VMEM((p.comp - 1, p.groups, p.beam, p.rows, p.length), BF16),
            pltpu.VMEM((p.rows * radix, radix), F32),
            pltpu.VMEM((2 * radix, 2 * radix), BF16),
            pltpu.VMEM((2 * radix, 2 * radix), BF16),
            pltpu.VMEM((2, radix, radix), F32),
            pltpu.VMEM((2 * radix, radix), F32),
            pltpu.VMEM((p.rows * radix, radix), F32),
            pltpu.VMEM((p.groups, radix, p.rows, radix), BF16),
            pltpu.VMEM((p.sub, p.slots, p.groups, p.share, p.rows, radix), BF16),
            pltpu.VMEM((2 * SIDE, p.padded), F32),
            pltpu.VMEM((p.slots, 2 * SIDE, p.padded), F32),
            pltpu.VMEM((p.padded, 128), F32),
            *[pltpu.VMEM((p.groups, n, 2, p.rows, p.length), BF16) for n in halves],
            *[pltpu.VMEM((p.groups, n, p.rows, p.length), BF16) for n in halves],
            *[pltpu.VMEM((2, 2, 2 * n, k), BF16) for n, k in zip(p.sizes, p.depths)],
            *[pltpu.VMEM((2, n, radix), F32) for n in p.sizes],
            *[pltpu.VMEM((2, 2, p.share, n, radix), F32) for n in p.sizes],
            pltpu.VMEM((p.comp, p.share, 2 * p.outs, radix), F32),
            pltpu.VMEM((p.comp, p.share, 2 * p.outs, radix), BF16),
            pltpu.VMEM((p.comp - 1, p.share, 2 * p.outs, radix), BF16),
            dma((PIECES,)),
            dma((8,)),
            dma((3 * p.comp,)),
            dma((p.comp + 1,)),
            dma((units * (p.comp - 1),)),
            dma((units * (p.comp - 1),)),
            dma((units * p.stages,)),
            dma((units * p.stages,)),
            dma((swap_count * len(p.swap_peers),)),
            dma((swap_count * len(p.swap_peers),)),
            dma((2 * swap_count,)),
            dma((2 * swap_count,)),
            dma(((p.comp - 1) * OUT_PIECES,)),
            dma(((p.comp - 1) * OUT_PIECES,)),
        ],
        compiler_params=pltpu.CompilerParams(
            collective_id=0, has_side_effects=True, vmem_limit_bytes=LIMIT
        ),
    )(
        angle, raw, filt, weights, offsets, delay, jnp.asarray(constants.T), jnp.asarray(constants.T),
        jnp.asarray(twiddle(radix)),
    )


def body(raw_pulses, range_filter, steer_angle, band_offsets, band_weights, beam_delay):
    counts = (lax.axis_size("sub"), lax.axis_size("beam"), lax.axis_size("comp"))
    columns = band_offsets.shape[1]
    plan = Plan(counts, steer_angle.shape, raw_pulses.shape[2], columns)
    radix = plan.radix
    filt = range_filter.reshape(2, radix, radix).transpose(1, 0, 2).reshape(2 * radix, radix)
    out = fused(
        plan, steer_angle, raw_pulses, filt, band_weights.transpose(0, 2, 1), band_offsets, beam_delay
    )
    out = store(out)
    out = out.reshape(plan.outs, plan.quarter, 2, radix).transpose(0, 2, 1, 3)
    return out.reshape(plan.outs, 2, plan.quarter * radix)


def solution(mesh):
    in_specs = (
        P(("sub", "beam", "comp"), None, None),
        P(),
        P(None, ("sub", "beam", "comp")),
        P(None, ("beam", "comp")),
        P(None, ("beam", "comp"), None),
        P(None, ("beam", "comp")),
    )
    out_specs = P(("beam", "comp"), None, "sub")
    return jax.shard_map(body, mesh=mesh, in_specs=in_specs, out_specs=out_specs, check_vma=False)
```

```python
import functools
import itertools
import math

import jax
import jax.numpy as jnp
import numpy as np
from jax import lax
from jax.experimental import pallas as pl
from jax.experimental.pallas import tpu as pltpu
from jax.sharding import PartitionSpec as P

BAND = 8
EXTRA = 8
SIDE = 12
GROUP = 2
PIECES = 4
LAG = 3
LAG_TWO = 2
LAST_PIECES = 4
BEAM_FIRST = (1, 5)
OUT_PIECES = 4
HALO_LAG = 2
LIMIT = 54 * 2**20
STORES = 4
MESH = pl.DeviceIdType.MESH
F32 = jnp.float32
BF16 = jnp.bfloat16


def dft_table(length):
    index_row = np.arange(length, dtype=np.int32)
    product = index_row[:, None] * index_row[None, :] % length
    phase_angle = product.astype(np.float32) * np.float32(2.0 * math.pi / length)
    return np.cos(phase_angle).astype(BF16), (-np.sin(phase_angle)).astype(BF16)


def real_form(length):
    cos_part, sin_part = dft_table(length)
    upper_rows = np.concatenate([cos_part, sin_part], axis=1)
    lower_rows = np.concatenate([-sin_part, cos_part], axis=1)
    return np.concatenate([upper_rows, lower_rows], axis=0)


def twiddle(radix):
    index_row = np.arange(radix, dtype=np.int32)
    product = index_row[:, None] * index_row[None, :] % (radix * radix)
    phase_angle = product.astype(np.float32) * np.float32(2.0 * math.pi / (radix * radix))
    return np.stack([np.cos(phase_angle), -np.sin(phase_angle)], 0).astype(np.float32)


def split(value):
    high = value.astype(BF16)
    return high, (value - high.astype(F32)).astype(BF16)


def dot(a, b):
    return jnp.dot(a, b, preferred_element_type=F32)


class Plan:
    def __init__(self, counts, angle_shape, length, columns):
        self.sub, self.beam, self.comp = counts
        self.blocks = self.beam * self.comp
        self.beams, self.pulses = angle_shape
        self.first = self.beams // self.blocks
        self.length = length
        self.radix = math.isqrt(length)
        self.columns = columns
        self.group = min(GROUP, self.first)
        self.groups = self.first // self.group
        self.rows = 2 * self.group
        self.counts = [PIECES] * (self.groups - 1) + [LAST_PIECES]
        self.units = [(g, h) for g in range(self.groups) for h in range(self.counts[g])]
        self.beam_first = [self.units[i] for i in BEAM_FIRST]
        self.levels = self.sub.bit_length() - 1
        self.quarter = self.radix // self.sub
        self.share = self.quarter // self.comp
        self.outs = self.first * self.sub
        self.padded = -(-columns // 128) * 128
        self.stages = self.beam.bit_length() - 1
        self.slots = self.comp + 2
        self.factor = float(self.pulses * self.blocks) ** (-0.5)
        self.sizes = []
        for level in range(self.levels):
            own = self.comp * self.first * 2 ** (level + 1)
            self.sizes.append(own + (0 if level == self.levels - 1 else 2 * EXTRA))
        self.depths = [2 * self.slots * self.first] + [2 * n for n in self.sizes[:-1]]
        near = {(0, d, e) for d in (-1, 0, 1) for e in range(self.comp)}
        near |= {(d, 0, e) for d in range(self.sub) for e in range(self.comp)}
        near |= {(0, d, 0) for d in range(self.beam)}
        self.peers = sorted({(d % self.sub, e % self.beam, f % self.comp) for d, e, f in near} - {(0, 0, 0)})
        need = BAND // 2
        for _ in range(self.levels - 1):
            need = (need + 1) // 2 + BAND // 2
        need = min(need, self.first) if self.comp > 1 else self.first
        self.edges = [g for g in range(self.groups) if g * self.group < need]
        self.swap_peers = [
            (d, e) for d in range(self.sub) for e in range(self.comp) if (d, e) != (0, 0)
        ]

    def pieces(self, level):
        new = self.first * 2 ** (level + 1)
        inner = [(k, 0, new) for k in range(self.comp)]
        if level == self.levels - 1:
            return inner
        return [(-1, new - EXTRA, EXTRA)] + inner + [(self.comp, 0, EXTRA)]


def fused_kernel(
    plan, angle_hbm, raw_hbm, filter_hbm, weights_hbm, offsets_hbm, delay_hbm, first_hbm,
    second_hbm, turn_hbm, out_ref, angle_ref, weights_ref, offsets_ref, delay_ref, raw, weight, part, recv_one, swap, first, second, turn, filt,
    blend, image, window, mine, tables, fields, *rest,
):
    p = plan
    levels = p.levels
    rest = list(rest)

    def take(number):
        taken = rest[:number]
        del rest[:number]
        return taken

    held, recv_two = take(p.stages), take(p.stages)
    wide_held, wide_recv = take(p.stages), take(p.stages)
    late_held, late_recv = take(2)
    lhs, delay, phase = take(levels), take(levels), take(levels)
    (final, outbound, inbound, load_sem, const_sem, table_send, table_recv, one_send, one_recv,
     two_send, two_recv, swap_send, swap_recv, halo_send, halo_recv, out_send, out_recv) = rest
    s = lax.axis_index("sub")
    b = lax.axis_index("beam")
    c = lax.axis_index("comp")
    has_low = b > 0
    has_high = b < p.beam - 1
    radix = p.radix

    def at(ds, db, dc):
        return {
            "sub": lax.rem(s + (ds % p.sub), p.sub),
            "beam": lax.rem(b + (db % p.beam), p.beam),
            "comp": lax.rem(c + (dc % p.comp), p.comp),
        }

    def remote(source, target, send, recv, place):
        return pltpu.make_async_remote_copy(
            src_ref=source, dst_ref=target, send_sem=send, recv_sem=recv, device_id=place,
            device_id_type=MESH,
        )

    angle_load = pltpu.make_async_copy(angle_hbm, angle_ref, const_sem.at[7])
    angle_load.start()
    def columns_of(g, h):
        width = p.length // p.counts[g]
        return pl.ds(h * width, width)

    loads = []
    for h in range(PIECES):
        cols = columns_of(0, h)
        loads.append(
            pltpu.make_async_copy(raw_hbm.at[:, :, cols], raw.at[:, :, cols], load_sem.at[h])
        )
        loads[h].start()
    constants = [
        pltpu.make_async_copy(source, target, const_sem.at[i])
        for i, (source, target) in enumerate(
            [
                (weights_hbm, weights_ref), (offsets_hbm, offsets_ref), (delay_hbm, delay_ref),
                (first_hbm, first), (second_hbm, second), (turn_hbm, turn), (filter_hbm, filt),
            ]
        )
    ]
    for copy in constants:
        copy.start()

    window[:, 0] = jnp.zeros(window.shape[:1] + window.shape[2:], BF16)
    window[:, p.comp + 1] = jnp.zeros(window.shape[:1] + window.shape[2:], BF16)
    barrier = pltpu.get_barrier_semaphore()
    for place in p.peers:
        pl.semaphore_signal(barrier, inc=1, device_id=at(*place), device_id_type=MESH)

    angle_load.wait()
    angle = angle_ref[...]
    cos_part = (jnp.cos(angle) * p.factor).astype(BF16)
    sin_part = (jnp.sin(angle) * p.factor).astype(BF16)
    stacked = jnp.concatenate(
        [
            jnp.concatenate([cos_part, -sin_part], axis=1),
            jnp.concatenate([sin_part, cos_part], axis=1),
        ],
        axis=0,
    )
    count, deep = 2 * p.beams, 2 * p.pulses
    source = lax.broadcasted_iota(jnp.int32, (deep, deep), 0)
    target = lax.broadcasted_iota(jnp.int32, (deep, deep), 1)
    place = jnp.where(source < p.pulses, 2 * source, 2 * (source - p.pulses) + 1)
    spread = jnp.where(place == target, 1.0, 0.0).astype(BF16)
    target = lax.broadcasted_iota(jnp.int32, (count, count), 0)
    source = lax.broadcasted_iota(jnp.int32, (count, count), 1)

    def bits(value, size):
        return jnp.bitwise_and(value, size - 1), lax.shift_right_logical(
            value, jnp.full_like(value, size.bit_length() - 1)
        )

    def order_of(group_at, comp_at):
        return jnp.where(comp_at == p.comp - 1, p.groups - 1 - group_at, group_at)

    within, upper = bits(target, p.group)
    half, upper = bits(upper, 2)
    beam_at, upper = bits(upper, p.beam)
    comp_at, group_at = bits(upper, p.comp)
    group_at = order_of(group_at, comp_at)
    origin = half * p.beams + (
        (beam_at * p.comp + comp_at) * p.first + group_at * p.group + within
    )
    order = jnp.where(origin == source, 1.0, 0.0).astype(BF16)
    weight[...] = dot(order, dot(stacked, spread).astype(BF16)).astype(BF16)

    def table_copy(db, dc):
        slot = 1 + c if db == 0 else (0 if db > 0 else p.comp + 1)
        k = (db + 1) * p.comp + dc
        r = dc if db == 0 else (0 if db > 0 else p.comp)
        return remote(mine, tables.at[slot], table_send.at[k], table_recv.at[r], at(0, db, dc))

    def table_ends(action):
        @pl.when(c == p.comp - 1)
        def _():
            for e in range(p.comp):
                action(table_copy(1, e))

        @pl.when(c == 0)
        def _():
            for e in range(p.comp):
                action(table_copy(-1, e))

    def send_tables():
        for copy in constants[:3]:
            copy.wait()
        mine[...] = jnp.zeros(mine.shape, F32)
        for side in range(2):
            row = side * SIDE
            mine[row : row + BAND, : p.columns] = weights_ref[side]
            mine[row + BAND : row + BAND + 1, : p.columns] = offsets_ref[side : side + 1].astype(F32)
            mine[row + BAND + 1 : row + BAND + 2, : p.columns] = delay_ref[side : side + 1]
        tables[1 + c] = mine[...]
        for e in range(1, p.comp):
            table_copy(0, e).start()
        table_ends(lambda copy: copy.start())

    one, two, swaps = {}, {}, {}

    def bit(stage):
        return lax.rem(lax.div(b, 2**stage), 2)

    def form(h):
        loads[h].wait()
        cols = columns_of(0, h)
        pulses = raw[:, :, cols].reshape(2 * p.pulses, -1)
        product = dot(weight[...], pulses).astype(BF16)
        part[:, :, :, :, :, cols] = product.reshape(
            p.groups, p.comp, p.beam // 2, 2, p.rows, -1
        )

    def partner(stage):
        return {"beam": b + (1 - 2 * bit(stage)) * 2**stage}

    def start_one(g, h):
        if (g, h) in p.beam_first:
            n = p.beam_first.index((g, h))
            return send_wide(0, n, part.at[g, :, :, 1 - bit(0), :, columns_of(g, h)])
        one[g, h] = []
        for d in range(1, p.comp):
            peer = lax.rem(c + d, p.comp)
            k = p.units.index((g, h)) * (p.comp - 1) + d - 1
            copy = remote(
                part.at[g, peer, :, :, :, columns_of(g, h)],
                recv_one.at[d - 1, g, :, :, :, columns_of(g, h)],
                one_send.at[k], one_recv.at[k], at(0, 0, d),
            )
            copy.start()
            one[g, h].append(copy)

    def send_wide(stage, n, source):
        k = p.units.index(p.beam_first[n]) * p.stages + stage
        copy = remote(
            source, wide_recv[stage].at[n], two_send.at[k], two_recv.at[k], partner(stage)
        )
        copy.start()
        two[(stage,) + p.beam_first[n]] = copy

    def gathered_wide(stage, n):
        g, h = p.beam_first[n]
        two[stage, g, h].wait_recv()
        if stage == 0:
            total = part[g, :, :, bit(0), :, columns_of(g, h)].astype(F32)
        else:
            total = wide_held[stage][n, :, :, bit(stage)].astype(F32)
        return total + wide_recv[stage][n].astype(F32)

    def step_wide(stage, n):
        total = gathered_wide(stage - 1, n)
        if stage < p.stages:
            wide_held[stage][n] = total.astype(BF16).reshape(wide_held[stage].shape[1:])
            return send_wide(stage, n, wide_held[stage].at[n, :, :, 1 - bit(stage)])
        g, h = p.beam_first[n]
        late_held[n] = total[:, 0].astype(BF16)
        one[g, h] = []
        for d in range(1, p.comp):
            k = p.units.index((g, h)) * (p.comp - 1) + d - 1
            copy = remote(
                late_held.at[n, lax.rem(c + d, p.comp)], late_recv.at[n, d - 1],
                one_send.at[k], one_recv.at[k], at(0, 0, d),
            )
            copy.start()
            one[g, h].append(copy)

    def send_two(stage, g, h, total):
        cols = columns_of(g, h)
        held[stage][g, :, :, :, cols] = total.astype(BF16).reshape(-1, 2, p.rows, cols.size)
        k = p.units.index((g, h)) * p.stages + stage
        copy = remote(
            held[stage].at[g, :, 1 - bit(stage), :, cols],
            recv_two[stage].at[g, :, :, cols],
            two_send.at[k], two_recv.at[k], partner(stage),
        )
        copy.start()
        two[stage, g, h] = copy

    def gathered(stage, g, h):
        cols = columns_of(g, h)
        two[stage, g, h].wait_recv()
        total = held[stage][g, :, bit(stage), :, cols].astype(F32)
        return total + recv_two[stage][g, :, :, cols].astype(F32)

    def step_beam(stage, g, h):
        if (g, h) in p.beam_first:
            return step_wide(stage + 1, p.beam_first.index((g, h)))
        if stage > 0:
            return send_two(stage, g, h, gathered(stage - 1, g, h))
        cols = columns_of(g, h)
        for copy in one[g, h]:
            copy.wait_recv()
        total = part[g, c, :, :, :, cols].astype(F32)
        for d in range(1, p.comp):
            total += recv_one[d - 1, g, :, :, :, cols].astype(F32)
        send_two(0, g, h, total)

    def finish(g, h):
        if (g, h) in p.beam_first:
            n = p.beam_first.index((g, h))
            total = late_held[n, c].astype(F32)
            for copy in one[g, h]:
                copy.wait_recv()
            for d in range(1, p.comp):
                total += late_recv[n, d - 1].astype(F32)
        else:
            total = gathered(p.stages - 1, g, h)[0]
        width = p.length // p.counts[g]
        for a in range(width // radix):
            swap[pl.ds(h * (width // radix) + a, p.rows, stride=radix), :] = total[
                :, a * radix : (a + 1) * radix
            ]

    deferred = []

    def compress(g, deferring):
        factor = p.length ** (-0.5)
        h_real = filt[pl.ds(0, radix, stride=2), :] * factor
        h_imag = filt[pl.ds(1, radix, stride=2), :] * factor
        span = p.group * radix

        @pl.loop(0, p.group // 2)
        def _(pair):
            sides = []
            for u in range(2):
                row = pl.multiple_of((2 * pair + u) * radix, radix)
                sides.append(
                    jnp.concatenate(
                        [swap[pl.ds(row, radix), :], swap[pl.ds(row + span, radix), :]], axis=0
                    )
                )
            high, low = split(jnp.concatenate(sides, axis=1))
            section = dot(first[...], high) + dot(first[...], low)
            cos_turn, sin_turn = turn[0], turn[1]
            turned = []
            for u in range(2):
                real = section[:radix, u * radix : (u + 1) * radix]
                imag = section[radix:, u * radix : (u + 1) * radix]
                turned.append(
                    jnp.concatenate(
                        [
                            real * cos_turn - imag * sin_turn,
                            real * sin_turn + imag * cos_turn,
                        ],
                        axis=1,
                    )
                )
            high, low = split(jnp.concatenate(turned, axis=0))
            both_last = (((1,), (1,)), ((), ()))
            spectrum = lax.dot_general(second[...], high, both_last, preferred_element_type=F32)
            spectrum += lax.dot_general(second[...], low, both_last, preferred_element_type=F32)
            for u in range(2):
                real = spectrum[:radix, u * radix : (u + 1) * radix]
                imag = spectrum[radix:, u * radix : (u + 1) * radix]
                row = 2 * pair + u
                blend[pl.ds(row, radix, stride=p.rows), :] = real * h_real - imag * h_imag
                blend[pl.ds(row + p.group, radix, stride=p.rows), :] = (
                    real * h_imag + imag * h_real
                )

        image[g] = blend[...].reshape(radix, p.rows, radix).astype(BF16)
        window[s, 1 + c, g] = image[g, pl.ds((s * p.comp + c) * p.share, p.share)]
        number = OUT_PIECES if g == p.groups - 1 else 1
        size = p.share // number
        for o in range(number):
            swaps[g, o] = []
            for i, (ds, dc) in enumerate(p.swap_peers):
                where = at(ds, 0, dc)
                begin = (where["sub"] * p.comp + where["comp"]) * p.share + o * size
                k = (g + o) * len(p.swap_peers) + i
                copy = remote(
                    image.at[g, pl.ds(begin, size)],
                    window.at[s, 1 + c, g, pl.ds(o * size, size)],
                    swap_send.at[k], swap_recv.at[k], where,
                )
                swaps[g, o].append(copy)
                if dc == 0 or not deferring:
                    copy.start()
                else:
                    deferred.append(copy)

    def halo_copy(g, o, step):
        near, far = (1, p.comp + 1) if step < 0 else (p.comp, 0)
        size = p.share // (OUT_PIECES if g == p.groups - 1 else 1)
        k = 2 * (g + o) + (0 if step < 0 else 1)
        return remote(
            window.at[:, near, g, pl.ds(o * size, size)],
            window.at[:, far, g, pl.ds(o * size, size)],
            halo_send.at[k], halo_recv.at[k], {"beam": b + step},
        )

    def start_halo(g, o=0):
        for copy in swaps[g, o]:
            copy.wait_recv()
        if g not in p.edges:
            return

        @pl.when(has_low)
        def _():
            halo_copy(g, o, -1).start()

        @pl.when(has_high)
        def _():
            halo_copy(g, o, 1).start()

    def wait_halo(g, o=0):
        if g not in p.edges:
            return

        @pl.when(has_low)
        def _():
            halo_copy(g, o, 1).wait_recv()
            halo_copy(g, o, -1).wait_send()

        @pl.when(has_high)
        def _():
            halo_copy(g, o, -1).wait_recv()
            halo_copy(g, o, 1).wait_send()

    def read_tables():
        for e in range(1, p.comp):
            table_copy(0, e).wait_recv()
        table_copy(1, 0).wait_recv()
        table_copy(-1, 0).wait_recv()
        for j in range(p.padded // 128):
            block = tables[:, :, j * 128 : (j + 1) * 128].reshape(-1, 128)
            short = 128 - block.shape[0]
            if short > 0:
                block = jnp.concatenate([block, jnp.zeros((short, 128), F32)], axis=0)
            fields[j * 128 : (j + 1) * 128, :] = block.T

    def fields_of(level, side):
        for step, begin, size in p.pieces(level):
            row = p.first * (2 ** (level + 1) - 2) + begin
            yield step, size, row, (step + 1) * 2 * SIDE + side * SIDE

    def build(level):
        depth, size = p.depths[level], p.sizes[level]
        child = p.first * 2**level
        lane = lax.broadcasted_iota(jnp.int32, (1, depth), 1)
        if level == 0:
            within, upper = bits(lane, p.group)
            half, upper = bits(upper, 2)
            group_at, slot = bits(upper, p.groups)
            comp_at = jnp.where(slot == 0, p.comp - 1, jnp.where(slot > p.comp, 0, slot - 1))
            group_at = order_of(group_at, comp_at)
            beam_at = slot * p.first + group_at * p.group + within
        else:
            half = jnp.where(lane < depth // 2, 0, 1)
            beam_at = lane - half * (depth // 2)
        begin = p.first if level == 0 else EXTRA
        for side in range(2):
            done = 0
            for step, rows, row, base in fields_of(level, side):
                block = fields[row : row + rows, base : base + SIDE]
                shift = block[:, BAND : BAND + 1].astype(jnp.int32)
                tap = beam_at - begin - step * child - shift
                band = jnp.zeros((rows, depth), F32)
                for t in range(BAND):
                    band += jnp.where(tap == t, block[:, t : t + 1], 0.0)
                if step < 0:
                    band = jnp.where(has_low, band, 0.0)
                if step >= p.comp:
                    band = jnp.where(has_high, band, 0.0)
                for r in range(2):
                    high, low = split(jnp.where(half == r, band, 0.0))
                    lhs[level][side, 0, r * size + done : r * size + done + rows, :] = high
                    lhs[level][side, 1, r * size + done : r * size + done + rows, :] = low
                delay[level][side, done : done + rows, :] = jnp.broadcast_to(
                    block[:, BAND + 1 : BAND + 2], (rows, radix)
                )
                done += rows

    def build_phases(begin, end):
        start = (s * p.comp + c) * p.share

        @pl.loop(begin, end)
        def _(m):
            for level in range(levels):
                for side in range(2):
                    factor = delay[level][side]
                    lane = lax.broadcasted_iota(jnp.int32, factor.shape, 1)
                    place = ((start + m) * radix + lane).astype(F32)
                    phase_angle = factor * (1.0 + place / p.length)
                    phase[level][0, side, m] = jnp.cos(phase_angle)
                    phase[level][1, side, m] = jnp.sin(phase_angle)

    def merge(m):
        def pair(load):
            return jnp.concatenate([load(m), load(m + 1)], axis=1)

        images = [
            pair(lambda k, i=i: window[i, :, :, k].reshape(p.depths[0], radix))
            for i in range(p.sub)
        ]
        for level in range(levels):
            size = p.sizes[level]
            merged = []
            for g in range(len(images) // 2):
                real, imag = 0.0, 0.0
                for side in range(2):
                    child = images[2 * g + side]
                    mixed = dot(lhs[level][side, 0], child) + dot(lhs[level][side, 1], child)
                    cosine = pair(lambda k: phase[level][0, side, k])
                    sine = pair(lambda k: phase[level][1, side, k])
                    real += cosine * mixed[:size] - sine * mixed[size:]
                    imag += sine * mixed[:size] + cosine * mixed[size:]
                merged.append((real, imag))
            if level + 1 < levels:
                images = [jnp.concatenate(parts, axis=0).astype(BF16) for parts in merged]
        for r in range(2):
            for k in range(p.comp):
                for u in range(2):
                    value = merged[0][r][k * p.outs : (k + 1) * p.outs, u * radix : (u + 1) * radix]
                    final[k, m + u, r * p.outs : (r + 1) * p.outs, :] = value
                    outbound[k, m + u, r * p.outs : (r + 1) * p.outs, :] = value.astype(BF16)

    def place_out(source, m, column):
        for r in range(2):
            value = source[r * p.outs : (r + 1) * p.outs].astype(F32)
            out_ref[pl.ds(2 * (column * p.share + m) + r, p.outs, stride=2 * p.quarter), :] = value

    units = p.units
    total_units = len(units)
    idle = range(PIECES, 2 * PIECES)
    per_step = -(-p.share // len(idle))
    pending = []
    last = p.groups - 1
    drain = LAG + LAG_TWO * p.stages
    form(0)
    pl.semaphore_wait(barrier, len(p.peers))
    for u in range(total_units + drain):
        if 0 < u < PIECES:
            form(u)
        if u < total_units:
            start_one(*units[u])
        if u == 1:
            send_tables()
        if u == total_units - 1:
            for copy in deferred:
                copy.start()
        for stage in range(p.stages):
            v = u - LAG - LAG_TWO * stage
            if 0 <= v < total_units:
                step_beam(stage, *units[v])
        v = u - drain
        while pending and v >= pending[0][0]:
            start_halo(pending.pop(0)[1])
        if u == PIECES:
            read_tables()
            for copy in constants[3:]:
                copy.wait()
            for level in range(levels):
                build(level)
        if u in idle:
            begin = min((u - PIECES) * per_step, p.share)
            end = min(begin + per_step, p.share)
            if end > begin:
                build_phases(begin, end)
        if v >= 0:
            finish(*units[v])
            g, h = units[v]
            if h == p.counts[g] - 1:
                compress(g, u < total_units - 1)
                if g < last:
                    pending.append((max(v + HALO_LAG, total_units - drain + 4), g))
    for _, g in pending:
        start_halo(g)
    for g in range(last):
        wait_halo(g)

    chunk = p.share // OUT_PIECES
    outs = []

    def merge_piece(o):
        @pl.loop(0, chunk // 2)
        def _(i):
            merge(o * chunk + 2 * i)

        for d in range(1, p.comp):
            peer = lax.rem(c + d, p.comp)
            k = (d - 1) * OUT_PIECES + o
            copy = remote(
                outbound.at[peer, pl.ds(o * chunk, chunk)],
                inbound.at[d - 1, pl.ds(o * chunk, chunk)],
                out_send.at[k], out_recv.at[k], at(0, 0, d),
            )
            copy.start()
            outs.append((o, d, copy))

    for o in range(OUT_PIECES):
        start_halo(last, o)
        if last not in p.edges:
            merge_piece(o)
    if last in p.edges:
        for o in range(OUT_PIECES):
            wait_halo(last, o)
            merge_piece(o)

    @pl.loop(0, p.share)
    def _(m):
        place_out(final[c, m], m, c)

    for o, d, copy in outs:
        copy.wait_recv()
        origin = lax.rem(c + p.comp - d, p.comp)

        @pl.loop(0, chunk)
        def _(i, o=o, d=d, origin=origin):
            place_out(inbound[d - 1, o * chunk + i], o * chunk + i, origin)

    for e in range(1, p.comp):
        table_copy(0, e).wait_send()
    table_ends(lambda copy: copy.wait_send())
    for copy in itertools.chain(
        *one.values(), two.values(), *swaps.values(), (entry[2] for entry in outs)
    ):
        copy.wait_send()


def store_kernel(value_ref, out_hbm, sem):
    size = value_ref.shape[0] // STORES
    copies = [
        pltpu.make_async_copy(
            value_ref.at[pl.ds(i * size, size)], out_hbm.at[pl.ds(i * size, size)], sem.at[i]
        )
        for i in range(STORES)
    ]
    for copy in copies:
        copy.start()
    for copy in copies:
        copy.wait()


def store(value):
    return pl.pallas_call(
        store_kernel,
        out_shape=jax.ShapeDtypeStruct(value.shape, value.dtype),
        in_specs=[pl.BlockSpec(memory_space=pltpu.VMEM)],
        out_specs=pl.BlockSpec(memory_space=pl.ANY),
        scratch_shapes=[pltpu.SemaphoreType.DMA((STORES,))],
        compiler_params=pltpu.CompilerParams(vmem_limit_bytes=8 * 2**20),
    )(value)


def fused(plan, angle, raw, filt, weights, offsets, delay):
    p = plan
    constants = real_form(p.radix)
    dma = pltpu.SemaphoreType.DMA
    radix = p.radix
    units = len(p.units)
    wide = p.length // PIECES
    early = len(p.beam_first)
    halves = [p.beam // 2 ** (t + 1) for t in range(p.stages)]
    swap_count = p.groups - 1 + OUT_PIECES
    return pl.pallas_call(
        functools.partial(fused_kernel, p),
        out_shape=pltpu.VMEM((p.outs * 2 * p.quarter, radix), F32),
        in_specs=[pl.BlockSpec(memory_space=pltpu.HBM)] * 9,
        out_specs=pl.BlockSpec(memory_space=pltpu.VMEM),
        scratch_shapes=[
            pltpu.VMEM(angle.shape, F32),
            pltpu.VMEM(weights.shape, F32),
            pltpu.VMEM(offsets.shape, jnp.int32),
            pltpu.VMEM(delay.shape, F32),
            pltpu.VMEM(raw.shape, BF16),
            pltpu.VMEM((2 * p.beams, 2 * p.pulses), BF16),
            pltpu.VMEM((p.groups, p.comp, p.beam // 2, 2, p.rows, p.length), BF16),
            pltpu.VMEM((p.comp - 1, p.groups, p.beam // 2, 2, p.rows, p.length), BF16),
            pltpu.VMEM((p.rows * radix, radix), F32),
            pltpu.VMEM((2 * radix, 2 * radix), BF16),
            pltpu.VMEM((2 * radix, 2 * radix), BF16),
            pltpu.VMEM((2, radix, radix), F32),
            pltpu.VMEM((2 * radix, radix), F32),
            pltpu.VMEM((p.rows * radix, radix), F32),
            pltpu.VMEM((p.groups, radix, p.rows, radix), BF16),
            pltpu.VMEM((p.sub, p.slots, p.groups, p.share, p.rows, radix), BF16),
            pltpu.VMEM((2 * SIDE, p.padded), F32),
            pltpu.VMEM((p.slots, 2 * SIDE, p.padded), F32),
            pltpu.VMEM((p.padded, 128), F32),
            *[pltpu.VMEM((p.groups, n, 2, p.rows, p.length), BF16) for n in halves],
            *[pltpu.VMEM((p.groups, n, p.rows, p.length), BF16) for n in halves],
            *[
                pltpu.VMEM((early, p.comp, n if t else 1, 2, p.rows, wide if t else 128), BF16)
                for t, n in enumerate(halves)
            ],
            *[pltpu.VMEM((early, p.comp, n, p.rows, wide), BF16) for n in halves],
            pltpu.VMEM((early, p.comp, p.rows, wide), BF16),
            pltpu.VMEM((early, p.comp - 1, p.rows, wide), BF16),
            *[pltpu.VMEM((2, 2, 2 * n, k), BF16) for n, k in zip(p.sizes, p.depths)],
            *[pltpu.VMEM((2, n, radix), F32) for n in p.sizes],
            *[pltpu.VMEM((2, 2, p.share, n, radix), F32) for n in p.sizes],
            pltpu.VMEM((p.comp, p.share, 2 * p.outs, radix), F32),
            pltpu.VMEM((p.comp, p.share, 2 * p.outs, radix), BF16),
            pltpu.VMEM((p.comp - 1, p.share, 2 * p.outs, radix), BF16),
            dma((PIECES,)),
            dma((8,)),
            dma((3 * p.comp,)),
            dma((p.comp + 1,)),
            dma((units * (p.comp - 1),)),
            dma((units * (p.comp - 1),)),
            dma((units * p.stages,)),
            dma((units * p.stages,)),
            dma((swap_count * len(p.swap_peers),)),
            dma((swap_count * len(p.swap_peers),)),
            dma((2 * swap_count,)),
            dma((2 * swap_count,)),
            dma(((p.comp - 1) * OUT_PIECES,)),
            dma(((p.comp - 1) * OUT_PIECES,)),
        ],
        compiler_params=pltpu.CompilerParams(
            collective_id=0, has_side_effects=True, vmem_limit_bytes=LIMIT
        ),
    )(
        angle, raw, filt, weights, offsets, delay, jnp.asarray(constants.T), jnp.asarray(constants.T),
        jnp.asarray(twiddle(radix)),
    )


def body(raw_pulses, range_filter, steer_angle, band_offsets, band_weights, beam_delay):
    counts = (lax.axis_size("sub"), lax.axis_size("beam"), lax.axis_size("comp"))
    columns = band_offsets.shape[1]
    plan = Plan(counts, steer_angle.shape, raw_pulses.shape[2], columns)
    radix = plan.radix
    filt = range_filter.reshape(2, radix, radix).transpose(1, 0, 2).reshape(2 * radix, radix)
    out = fused(
        plan, steer_angle, raw_pulses, filt, band_weights.transpose(0, 2, 1), band_offsets, beam_delay
    )
    out = store(out)
    out = out.reshape(plan.outs, plan.quarter, 2, radix).transpose(0, 2, 1, 3)
    return out.reshape(plan.outs, 2, plan.quarter * radix)


def solution(mesh):
    in_specs = (
        P(("sub", "beam", "comp"), None, None),
        P(),
        P(None, ("sub", "beam", "comp")),
        P(None, ("beam", "comp")),
        P(None, ("beam", "comp"), None),
        P(None, ("beam", "comp")),
    )
    out_specs = P(("beam", "comp"), None, "sub")
    return jax.shard_map(body, mesh=mesh, in_specs=in_specs, out_specs=out_specs, check_vma=False)
```

```python
import functools
import itertools
import math

import jax
import jax.numpy as jnp
import numpy as np
from jax import lax
from jax.experimental import pallas as pl
from jax.experimental.pallas import tpu as pltpu
from jax.sharding import PartitionSpec as P

BAND = 8
EXTRA = 8
SIDE = 12
GROUP = 2
PIECES = 4
LAG = 3
LAG_TWO = 2
LAST_PIECES = 4
BEAM_FIRST = (1, 4, 7, 10)
OUT_PIECES = 4
HALO_LAG = 2
LIMIT = 54 * 2**20
STORES = 4
MESH = pl.DeviceIdType.MESH
F32 = jnp.float32
BF16 = jnp.bfloat16


def dft_table(length):
    index_row = np.arange(length, dtype=np.int32)
    product = index_row[:, None] * index_row[None, :] % length
    phase_angle = product.astype(np.float32) * np.float32(2.0 * math.pi / length)
    return np.cos(phase_angle).astype(BF16), (-np.sin(phase_angle)).astype(BF16)


def real_form(length):
    cos_part, sin_part = dft_table(length)
    upper_rows = np.concatenate([cos_part, sin_part], axis=1)
    lower_rows = np.concatenate([-sin_part, cos_part], axis=1)
    return np.concatenate([upper_rows, lower_rows], axis=0)


def twiddle(radix):
    index_row = np.arange(radix, dtype=np.int32)
    product = index_row[:, None] * index_row[None, :] % (radix * radix)
    phase_angle = product.astype(np.float32) * np.float32(2.0 * math.pi / (radix * radix))
    return np.stack([np.cos(phase_angle), -np.sin(phase_angle)], 0).astype(np.float32)


def split(value):
    high = value.astype(BF16)
    return high, (value - high.astype(F32)).astype(BF16)


def dot(a, b):
    return jnp.dot(a, b, preferred_element_type=F32)


class Plan:
    def __init__(self, counts, angle_shape, length, columns):
        self.sub, self.beam, self.comp = counts
        self.blocks = self.beam * self.comp
        self.beams, self.pulses = angle_shape
        self.first = self.beams // self.blocks
        self.length = length
        self.radix = math.isqrt(length)
        self.columns = columns
        self.group = min(GROUP, self.first)
        self.groups = self.first // self.group
        self.rows = 2 * self.group
        self.counts = [PIECES] * (self.groups - 1) + [LAST_PIECES]
        self.units = [(g, h) for g in range(self.groups) for h in range(self.counts[g])]
        self.beam_first = [self.units[i] for i in BEAM_FIRST]
        self.levels = self.sub.bit_length() - 1
        self.quarter = self.radix // self.sub
        self.share = self.quarter // self.comp
        self.outs = self.first * self.sub
        self.padded = -(-columns // 128) * 128
        self.stages = self.beam.bit_length() - 1
        self.slots = self.comp + 2
        self.factor = float(self.pulses * self.blocks) ** (-0.5)
        self.sizes = []
        for level in range(self.levels):
            own = self.comp * self.first * 2 ** (level + 1)
            self.sizes.append(own + (0 if level == self.levels - 1 else 2 * EXTRA))
        self.depths = [2 * self.slots * self.first] + [2 * n for n in self.sizes[:-1]]
        near = {(0, d, e) for d in (-1, 0, 1) for e in range(self.comp)}
        near |= {(d, 0, e) for d in range(self.sub) for e in range(self.comp)}
        near |= {(0, d, 0) for d in range(self.beam)}
        self.peers = sorted({(d % self.sub, e % self.beam, f % self.comp) for d, e, f in near} - {(0, 0, 0)})
        need = BAND // 2
        for _ in range(self.levels - 1):
            need = (need + 1) // 2 + BAND // 2
        need = min(need, self.first) if self.comp > 1 else self.first
        self.edges = [g for g in range(self.groups) if g * self.group < need]
        self.swap_peers = [
            (d, e) for d in range(self.sub) for e in range(self.comp) if (d, e) != (0, 0)
        ]

    def pieces(self, level):
        new = self.first * 2 ** (level + 1)
        inner = [(k, 0, new) for k in range(self.comp)]
        if level == self.levels - 1:
            return inner
        return [(-1, new - EXTRA, EXTRA)] + inner + [(self.comp, 0, EXTRA)]


def fused_kernel(
    plan, angle_hbm, raw_hbm, filter_hbm, weights_hbm, offsets_hbm, delay_hbm, first_hbm,
    second_hbm, turn_hbm, out_ref, angle_ref, weights_ref, offsets_ref, delay_ref, raw, weight, part, recv_one, swap, first, second, turn, filt,
    blend, image, window, mine, tables, fields, *rest,
):
    p = plan
    levels = p.levels
    rest = list(rest)

    def take(number):
        taken = rest[:number]
        del rest[:number]
        return taken

    held, recv_two = take(p.stages), take(p.stages)
    wide_held, wide_recv = take(p.stages), take(p.stages)
    late_held, late_recv = take(2)
    lhs, delay, phase = take(levels), take(levels), take(levels)
    (final, outbound, inbound, load_sem, const_sem, table_send, table_recv, one_send, one_recv,
     two_send, two_recv, swap_send, swap_recv, halo_send, halo_recv, out_send, out_recv) = rest
    s = lax.axis_index("sub")
    b = lax.axis_index("beam")
    c = lax.axis_index("comp")
    has_low = b > 0
    has_high = b < p.beam - 1
    radix = p.radix

    def at(ds, db, dc):
        return {
            "sub": lax.rem(s + (ds % p.sub), p.sub),
            "beam": lax.rem(b + (db % p.beam), p.beam),
            "comp": lax.rem(c + (dc % p.comp), p.comp),
        }

    def remote(source, target, send, recv, place):
        return pltpu.make_async_remote_copy(
            src_ref=source, dst_ref=target, send_sem=send, recv_sem=recv, device_id=place,
            device_id_type=MESH,
        )

    angle_load = pltpu.make_async_copy(angle_hbm, angle_ref, const_sem.at[7])
    angle_load.start()
    def columns_of(g, h):
        width = p.length // p.counts[g]
        return pl.ds(h * width, width)

    loads = []
    for h in range(PIECES):
        cols = columns_of(0, h)
        loads.append(
            pltpu.make_async_copy(raw_hbm.at[:, :, cols], raw.at[:, :, cols], load_sem.at[h])
        )
        loads[h].start()
    constants = [
        pltpu.make_async_copy(source, target, const_sem.at[i])
        for i, (source, target) in enumerate(
            [
                (weights_hbm, weights_ref), (offsets_hbm, offsets_ref), (delay_hbm, delay_ref),
                (first_hbm, first), (second_hbm, second), (turn_hbm, turn), (filter_hbm, filt),
            ]
        )
    ]
    for copy in constants:
        copy.start()

    window[:, 0] = jnp.zeros(window.shape[:1] + window.shape[2:], BF16)
    window[:, p.comp + 1] = jnp.zeros(window.shape[:1] + window.shape[2:], BF16)
    barrier = pltpu.get_barrier_semaphore()
    for place in p.peers:
        pl.semaphore_signal(barrier, inc=1, device_id=at(*place), device_id_type=MESH)

    angle_load.wait()
    angle = angle_ref[...]
    cos_part = (jnp.cos(angle) * p.factor).astype(BF16)
    sin_part = (jnp.sin(angle) * p.factor).astype(BF16)
    stacked = jnp.concatenate(
        [
            jnp.concatenate([cos_part, -sin_part], axis=1),
            jnp.concatenate([sin_part, cos_part], axis=1),
        ],
        axis=0,
    )
    count, deep = 2 * p.beams, 2 * p.pulses
    source = lax.broadcasted_iota(jnp.int32, (deep, deep), 0)
    target = lax.broadcasted_iota(jnp.int32, (deep, deep), 1)
    place = jnp.where(source < p.pulses, 2 * source, 2 * (source - p.pulses) + 1)
    spread = jnp.where(place == target, 1.0, 0.0).astype(BF16)
    target = lax.broadcasted_iota(jnp.int32, (count, count), 0)
    source = lax.broadcasted_iota(jnp.int32, (count, count), 1)

    def bits(value, size):
        return jnp.bitwise_and(value, size - 1), lax.shift_right_logical(
            value, jnp.full_like(value, size.bit_length() - 1)
        )

    def order_of(group_at, comp_at):
        return jnp.where(comp_at == p.comp - 1, p.groups - 1 - group_at, group_at)

    within, upper = bits(target, p.group)
    half, upper = bits(upper, 2)
    beam_at, upper = bits(upper, p.beam)
    comp_at, group_at = bits(upper, p.comp)
    group_at = order_of(group_at, comp_at)
    origin = half * p.beams + (
        (beam_at * p.comp + comp_at) * p.first + group_at * p.group + within
    )
    order = jnp.where(origin == source, 1.0, 0.0).astype(BF16)
    weight[...] = dot(order, dot(stacked, spread).astype(BF16)).astype(BF16)

    def table_copy(db, dc):
        slot = 1 + c if db == 0 else (0 if db > 0 else p.comp + 1)
        k = (db + 1) * p.comp + dc
        r = dc if db == 0 else (0 if db > 0 else p.comp)
        return remote(mine, tables.at[slot], table_send.at[k], table_recv.at[r], at(0, db, dc))

    def table_ends(action):
        @pl.when(c == p.comp - 1)
        def _():
            for e in range(p.comp):
                action(table_copy(1, e))

        @pl.when(c == 0)
        def _():
            for e in range(p.comp):
                action(table_copy(-1, e))

    def send_tables():
        for copy in constants[:3]:
            copy.wait()
        mine[...] = jnp.zeros(mine.shape, F32)
        for side in range(2):
            row = side * SIDE
            mine[row : row + BAND, : p.columns] = weights_ref[side]
            mine[row + BAND : row + BAND + 1, : p.columns] = offsets_ref[side : side + 1].astype(F32)
            mine[row + BAND + 1 : row + BAND + 2, : p.columns] = delay_ref[side : side + 1]
        tables[1 + c] = mine[...]
        for e in range(1, p.comp):
            table_copy(0, e).start()
        table_ends(lambda copy: copy.start())

    one, two, swaps = {}, {}, {}

    def bit(stage):
        return lax.rem(lax.div(b, 2**stage), 2)

    def form(h):
        loads[h].wait()
        cols = columns_of(0, h)
        pulses = raw[:, :, cols].reshape(2 * p.pulses, -1)
        product = dot(weight[...], pulses).astype(BF16)
        part[:, :, :, :, :, cols] = product.reshape(
            p.groups, p.comp, p.beam // 2, 2, p.rows, -1
        )

    def partner(stage):
        return {"beam": b + (1 - 2 * bit(stage)) * 2**stage}

    def start_one(g, h):
        if (g, h) in p.beam_first:
            n = p.beam_first.index((g, h))
            return send_wide(0, n, part.at[g, :, :, 1 - bit(0), :, columns_of(g, h)])
        one[g, h] = []
        for d in range(1, p.comp):
            peer = lax.rem(c + d, p.comp)
            k = p.units.index((g, h)) * (p.comp - 1) + d - 1
            copy = remote(
                part.at[g, peer, :, :, :, columns_of(g, h)],
                recv_one.at[d - 1, g, :, :, :, columns_of(g, h)],
                one_send.at[k], one_recv.at[k], at(0, 0, d),
            )
            copy.start()
            one[g, h].append(copy)

    def send_wide(stage, n, source):
        k = p.units.index(p.beam_first[n]) * p.stages + stage
        copy = remote(
            source, wide_recv[stage].at[n], two_send.at[k], two_recv.at[k], partner(stage)
        )
        copy.start()
        two[(stage,) + p.beam_first[n]] = copy

    def gathered_wide(stage, n):
        g, h = p.beam_first[n]
        two[stage, g, h].wait_recv()
        if stage == 0:
            total = part[g, :, :, bit(0), :, columns_of(g, h)].astype(F32)
        else:
            total = wide_held[stage][n, :, :, bit(stage)].astype(F32)
        return total + wide_recv[stage][n].astype(F32)

    def step_wide(stage, n):
        total = gathered_wide(stage - 1, n)
        if stage < p.stages:
            wide_held[stage][n] = total.astype(BF16).reshape(wide_held[stage].shape[1:])
            return send_wide(stage, n, wide_held[stage].at[n, :, :, 1 - bit(stage)])
        g, h = p.beam_first[n]
        late_held[n] = total[:, 0].astype(BF16)
        one[g, h] = []
        for d in range(1, p.comp):
            k = p.units.index((g, h)) * (p.comp - 1) + d - 1
            copy = remote(
                late_held.at[n, lax.rem(c + d, p.comp)], late_recv.at[n, d - 1],
                one_send.at[k], one_recv.at[k], at(0, 0, d),
            )
            copy.start()
            one[g, h].append(copy)

    def send_two(stage, g, h, total):
        cols = columns_of(g, h)
        held[stage][g, :, :, :, cols] = total.astype(BF16).reshape(-1, 2, p.rows, cols.size)
        k = p.units.index((g, h)) * p.stages + stage
        copy = remote(
            held[stage].at[g, :, 1 - bit(stage), :, cols],
            recv_two[stage].at[g, :, :, cols],
            two_send.at[k], two_recv.at[k], partner(stage),
        )
        copy.start()
        two[stage, g, h] = copy

    def gathered(stage, g, h):
        cols = columns_of(g, h)
        two[stage, g, h].wait_recv()
        total = held[stage][g, :, bit(stage), :, cols].astype(F32)
        return total + recv_two[stage][g, :, :, cols].astype(F32)

    def step_beam(stage, g, h):
        if (g, h) in p.beam_first:
            return step_wide(stage + 1, p.beam_first.index((g, h)))
        if stage > 0:
            return send_two(stage, g, h, gathered(stage - 1, g, h))
        cols = columns_of(g, h)
        for copy in one[g, h]:
            copy.wait_recv()
        total = part[g, c, :, :, :, cols].astype(F32)
        for d in range(1, p.comp):
            total += recv_one[d - 1, g, :, :, :, cols].astype(F32)
        send_two(0, g, h, total)

    def finish(g, h):
        if (g, h) in p.beam_first:
            n = p.beam_first.index((g, h))
            total = late_held[n, c].astype(F32)
            for copy in one[g, h]:
                copy.wait_recv()
            for d in range(1, p.comp):
                total += late_recv[n, d - 1].astype(F32)
        else:
            total = gathered(p.stages - 1, g, h)[0]
        width = p.length // p.counts[g]
        for a in range(width // radix):
            swap[pl.ds(h * (width // radix) + a, p.rows, stride=radix), :] = total[
                :, a * radix : (a + 1) * radix
            ]

    deferred = []

    def compress(g, deferring):
        factor = p.length ** (-0.5)
        h_real = filt[pl.ds(0, radix, stride=2), :] * factor
        h_imag = filt[pl.ds(1, radix, stride=2), :] * factor
        span = p.group * radix

        @pl.loop(0, p.group // 2)
        def _(pair):
            sides = []
            for u in range(2):
                row = pl.multiple_of((2 * pair + u) * radix, radix)
                sides.append(
                    jnp.concatenate(
                        [swap[pl.ds(row, radix), :], swap[pl.ds(row + span, radix), :]], axis=0
                    )
                )
            high, low = split(jnp.concatenate(sides, axis=1))
            section = dot(first[...], high) + dot(first[...], low)
            cos_turn, sin_turn = turn[0], turn[1]
            turned = []
            for u in range(2):
                real = section[:radix, u * radix : (u + 1) * radix]
                imag = section[radix:, u * radix : (u + 1) * radix]
                turned.append(
                    jnp.concatenate(
                        [
                            real * cos_turn - imag * sin_turn,
                            real * sin_turn + imag * cos_turn,
                        ],
                        axis=1,
                    )
                )
            high, low = split(jnp.concatenate(turned, axis=0))
            both_last = (((1,), (1,)), ((), ()))
            spectrum = lax.dot_general(second[...], high, both_last, preferred_element_type=F32)
            spectrum += lax.dot_general(second[...], low, both_last, preferred_element_type=F32)
            for u in range(2):
                real = spectrum[:radix, u * radix : (u + 1) * radix]
                imag = spectrum[radix:, u * radix : (u + 1) * radix]
                row = 2 * pair + u
                blend[pl.ds(row, radix, stride=p.rows), :] = real * h_real - imag * h_imag
                blend[pl.ds(row + p.group, radix, stride=p.rows), :] = (
                    real * h_imag + imag * h_real
                )

        image[g] = blend[...].reshape(radix, p.rows, radix).astype(BF16)
        window[s, 1 + c, g] = image[g, pl.ds((s * p.comp + c) * p.share, p.share)]
        number = OUT_PIECES if g == p.groups - 1 else 1
        size = p.share // number
        for o in range(number):
            swaps[g, o] = []
            for i, (ds, dc) in enumerate(p.swap_peers):
                where = at(ds, 0, dc)
                begin = (where["sub"] * p.comp + where["comp"]) * p.share + o * size
                k = (g + o) * len(p.swap_peers) + i
                copy = remote(
                    image.at[g, pl.ds(begin, size)],
                    window.at[s, 1 + c, g, pl.ds(o * size, size)],
                    swap_send.at[k], swap_recv.at[k], where,
                )
                swaps[g, o].append(copy)
                if dc == 0 or not deferring:
                    copy.start()
                else:
                    deferred.append(copy)

    def halo_copy(g, o, step):
        near, far = (1, p.comp + 1) if step < 0 else (p.comp, 0)
        size = p.share // (OUT_PIECES if g == p.groups - 1 else 1)
        k = 2 * (g + o) + (0 if step < 0 else 1)
        return remote(
            window.at[:, near, g, pl.ds(o * size, size)],
            window.at[:, far, g, pl.ds(o * size, size)],
            halo_send.at[k], halo_recv.at[k], {"beam": b + step},
        )

    def start_halo(g, o=0):
        for copy in swaps[g, o]:
            copy.wait_recv()
        if g not in p.edges:
            return

        @pl.when(has_low)
        def _():
            halo_copy(g, o, -1).start()

        @pl.when(has_high)
        def _():
            halo_copy(g, o, 1).start()

    def wait_halo(g, o=0):
        if g not in p.edges:
            return

        @pl.when(has_low)
        def _():
            halo_copy(g, o, 1).wait_recv()
            halo_copy(g, o, -1).wait_send()

        @pl.when(has_high)
        def _():
            halo_copy(g, o, -1).wait_recv()
            halo_copy(g, o, 1).wait_send()

    def read_tables():
        for e in range(1, p.comp):
            table_copy(0, e).wait_recv()
        table_copy(1, 0).wait_recv()
        table_copy(-1, 0).wait_recv()
        for j in range(p.padded // 128):
            block = tables[:, :, j * 128 : (j + 1) * 128].reshape(-1, 128)
            short = 128 - block.shape[0]
            if short > 0:
                block = jnp.concatenate([block, jnp.zeros((short, 128), F32)], axis=0)
            fields[j * 128 : (j + 1) * 128, :] = block.T

    def fields_of(level, side):
        for step, begin, size in p.pieces(level):
            row = p.first * (2 ** (level + 1) - 2) + begin
            yield step, size, row, (step + 1) * 2 * SIDE + side * SIDE

    def build(level):
        depth, size = p.depths[level], p.sizes[level]
        child = p.first * 2**level
        lane = lax.broadcasted_iota(jnp.int32, (1, depth), 1)
        if level == 0:
            within, upper = bits(lane, p.group)
            half, upper = bits(upper, 2)
            group_at, slot = bits(upper, p.groups)
            comp_at = jnp.where(slot == 0, p.comp - 1, jnp.where(slot > p.comp, 0, slot - 1))
            group_at = order_of(group_at, comp_at)
            beam_at = slot * p.first + group_at * p.group + within
        else:
            half = jnp.where(lane < depth // 2, 0, 1)
            beam_at = lane - half * (depth // 2)
        begin = p.first if level == 0 else EXTRA
        for side in range(2):
            done = 0
            for step, rows, row, base in fields_of(level, side):
                block = fields[row : row + rows, base : base + SIDE]
                shift = block[:, BAND : BAND + 1].astype(jnp.int32)
                tap = beam_at - begin - step * child - shift
                band = jnp.zeros((rows, depth), F32)
                for t in range(BAND):
                    band += jnp.where(tap == t, block[:, t : t + 1], 0.0)
                if step < 0:
                    band = jnp.where(has_low, band, 0.0)
                if step >= p.comp:
                    band = jnp.where(has_high, band, 0.0)
                for r in range(2):
                    high, low = split(jnp.where(half == r, band, 0.0))
                    lhs[level][side, 0, r * size + done : r * size + done + rows, :] = high
                    lhs[level][side, 1, r * size + done : r * size + done + rows, :] = low
                delay[level][side, done : done + rows, :] = jnp.broadcast_to(
                    block[:, BAND + 1 : BAND + 2], (rows, radix)
                )
                done += rows

    def build_phases(begin, end):
        start = (s * p.comp + c) * p.share

        @pl.loop(begin, end)
        def _(m):
            for level in range(levels):
                for side in range(2):
                    factor = delay[level][side]
                    lane = lax.broadcasted_iota(jnp.int32, factor.shape, 1)
                    place = ((start + m) * radix + lane).astype(F32)
                    phase_angle = factor * (1.0 + place / p.length)
                    phase[level][0, side, m] = jnp.cos(phase_angle)
                    phase[level][1, side, m] = jnp.sin(phase_angle)

    def merge(m):
        def pair(load):
            return jnp.concatenate([load(m), load(m + 1)], axis=1)

        images = [
            pair(lambda k, i=i: window[i, :, :, k].reshape(p.depths[0], radix))
            for i in range(p.sub)
        ]
        for level in range(levels):
            size = p.sizes[level]
            merged = []
            for g in range(len(images) // 2):
                real, imag = 0.0, 0.0
                for side in range(2):
                    child = images[2 * g + side]
                    mixed = dot(lhs[level][side, 0], child) + dot(lhs[level][side, 1], child)
                    cosine = pair(lambda k: phase[level][0, side, k])
                    sine = pair(lambda k: phase[level][1, side, k])
                    real += cosine * mixed[:size] - sine * mixed[size:]
                    imag += sine * mixed[:size] + cosine * mixed[size:]
                merged.append((real, imag))
            if level + 1 < levels:
                images = [jnp.concatenate(parts, axis=0).astype(BF16) for parts in merged]
        for r in range(2):
            for k in range(p.comp):
                for u in range(2):
                    value = merged[0][r][k * p.outs : (k + 1) * p.outs, u * radix : (u + 1) * radix]
                    final[k, m + u, r * p.outs : (r + 1) * p.outs, :] = value
                    outbound[k, m + u, r * p.outs : (r + 1) * p.outs, :] = value.astype(BF16)

    def place_out(source, m, column):
        for r in range(2):
            value = source[r * p.outs : (r + 1) * p.outs].astype(F32)
            out_ref[pl.ds(2 * (column * p.share + m) + r, p.outs, stride=2 * p.quarter), :] = value

    units = p.units
    total_units = len(units)
    idle = range(PIECES, 2 * PIECES)
    per_step = -(-p.share // len(idle))
    pending = []
    last = p.groups - 1
    drain = LAG + LAG_TWO * p.stages
    form(0)
    pl.semaphore_wait(barrier, len(p.peers))
    for u in range(total_units + drain):
        if 0 < u < PIECES:
            form(u)
        if u < total_units:
            start_one(*units[u])
        if u == 1:
            send_tables()
        if u == total_units - 1:
            for copy in deferred:
                copy.start()
        for stage in range(p.stages):
            v = u - LAG - LAG_TWO * stage
            if 0 <= v < total_units:
                step_beam(stage, *units[v])
        v = u - drain
        while pending and v >= pending[0][0]:
            start_halo(pending.pop(0)[1])
        if u == PIECES:
            read_tables()
            for copy in constants[3:]:
                copy.wait()
            for level in range(levels):
                build(level)
        if u in idle:
            begin = min((u - PIECES) * per_step, p.share)
            end = min(begin + per_step, p.share)
            if end > begin:
                build_phases(begin, end)
        if v >= 0:
            finish(*units[v])
            g, h = units[v]
            if h == p.counts[g] - 1:
                compress(g, u < total_units - 1)
                if g < last:
                    pending.append((max(v + HALO_LAG, total_units - drain + 4), g))
    for _, g in pending:
        start_halo(g)
    for g in range(last):
        wait_halo(g)

    chunk = p.share // OUT_PIECES
    outs = []

    def merge_piece(o):
        @pl.loop(0, chunk // 2)
        def _(i):
            merge(o * chunk + 2 * i)

        for d in range(1, p.comp):
            peer = lax.rem(c + d, p.comp)
            k = (d - 1) * OUT_PIECES + o
            copy = remote(
                outbound.at[peer, pl.ds(o * chunk, chunk)],
                inbound.at[d - 1, pl.ds(o * chunk, chunk)],
                out_send.at[k], out_recv.at[k], at(0, 0, d),
            )
            copy.start()
            outs.append((o, d, copy))

    for o in range(OUT_PIECES):
        start_halo(last, o)
        if last not in p.edges:
            merge_piece(o)
    if last in p.edges:
        for o in range(OUT_PIECES):
            wait_halo(last, o)
            merge_piece(o)

    @pl.loop(0, p.share)
    def _(m):
        place_out(final[c, m], m, c)

    for o, d, copy in outs:
        copy.wait_recv()
        origin = lax.rem(c + p.comp - d, p.comp)

        @pl.loop(0, chunk)
        def _(i, o=o, d=d, origin=origin):
            place_out(inbound[d - 1, o * chunk + i], o * chunk + i, origin)

    for e in range(1, p.comp):
        table_copy(0, e).wait_send()
    table_ends(lambda copy: copy.wait_send())
    for copy in itertools.chain(
        *one.values(), two.values(), *swaps.values(), (entry[2] for entry in outs)
    ):
        copy.wait_send()


def store_kernel(value_ref, out_hbm, sem):
    size = value_ref.shape[0] // STORES
    copies = [
        pltpu.make_async_copy(
            value_ref.at[pl.ds(i * size, size)], out_hbm.at[pl.ds(i * size, size)], sem.at[i]
        )
        for i in range(STORES)
    ]
    for copy in copies:
        copy.start()
    for copy in copies:
        copy.wait()


def store(value):
    return pl.pallas_call(
        store_kernel,
        out_shape=jax.ShapeDtypeStruct(value.shape, value.dtype),
        in_specs=[pl.BlockSpec(memory_space=pltpu.VMEM)],
        out_specs=pl.BlockSpec(memory_space=pl.ANY),
        scratch_shapes=[pltpu.SemaphoreType.DMA((STORES,))],
        compiler_params=pltpu.CompilerParams(vmem_limit_bytes=8 * 2**20),
    )(value)


def fused(plan, angle, raw, filt, weights, offsets, delay):
    p = plan
    constants = real_form(p.radix)
    dma = pltpu.SemaphoreType.DMA
    radix = p.radix
    units = len(p.units)
    wide = p.length // PIECES
    early = len(p.beam_first)
    halves = [p.beam // 2 ** (t + 1) for t in range(p.stages)]
    swap_count = p.groups - 1 + OUT_PIECES
    return pl.pallas_call(
        functools.partial(fused_kernel, p),
        out_shape=pltpu.VMEM((p.outs * 2 * p.quarter, radix), F32),
        in_specs=[pl.BlockSpec(memory_space=pltpu.HBM)] * 9,
        out_specs=pl.BlockSpec(memory_space=pltpu.VMEM),
        scratch_shapes=[
            pltpu.VMEM(angle.shape, F32),
            pltpu.VMEM(weights.shape, F32),
            pltpu.VMEM(offsets.shape, jnp.int32),
            pltpu.VMEM(delay.shape, F32),
            pltpu.VMEM(raw.shape, BF16),
            pltpu.VMEM((2 * p.beams, 2 * p.pulses), BF16),
            pltpu.VMEM((p.groups, p.comp, p.beam // 2, 2, p.rows, p.length), BF16),
            pltpu.VMEM((p.comp - 1, p.groups, p.beam // 2, 2, p.rows, p.length), BF16),
            pltpu.VMEM((p.rows * radix, radix), F32),
            pltpu.VMEM((2 * radix, 2 * radix), BF16),
            pltpu.VMEM((2 * radix, 2 * radix), BF16),
            pltpu.VMEM((2, radix, radix), F32),
            pltpu.VMEM((2 * radix, radix), F32),
            pltpu.VMEM((p.rows * radix, radix), F32),
            pltpu.VMEM((p.groups, radix, p.rows, radix), BF16),
            pltpu.VMEM((p.sub, p.slots, p.groups, p.share, p.rows, radix), BF16),
            pltpu.VMEM((2 * SIDE, p.padded), F32),
            pltpu.VMEM((p.slots, 2 * SIDE, p.padded), F32),
            pltpu.VMEM((p.padded, 128), F32),
            *[pltpu.VMEM((p.groups, n, 2, p.rows, p.length), BF16) for n in halves],
            *[pltpu.VMEM((p.groups, n, p.rows, p.length), BF16) for n in halves],
            *[
                pltpu.VMEM((early, p.comp, n if t else 1, 2, p.rows, wide if t else 128), BF16)
                for t, n in enumerate(halves)
            ],
            *[pltpu.VMEM((early, p.comp, n, p.rows, wide), BF16) for n in halves],
            pltpu.VMEM((early, p.comp, p.rows, wide), BF16),
            pltpu.VMEM((early, p.comp - 1, p.rows, wide), BF16),
            *[pltpu.VMEM((2, 2, 2 * n, k), BF16) for n, k in zip(p.sizes, p.depths)],
            *[pltpu.VMEM((2, n, radix), F32) for n in p.sizes],
            *[pltpu.VMEM((2, 2, p.share, n, radix), F32) for n in p.sizes],
            pltpu.VMEM((p.comp, p.share, 2 * p.outs, radix), F32),
            pltpu.VMEM((p.comp, p.share, 2 * p.outs, radix), BF16),
            pltpu.VMEM((p.comp - 1, p.share, 2 * p.outs, radix), BF16),
            dma((PIECES,)),
            dma((8,)),
            dma((3 * p.comp,)),
            dma((p.comp + 1,)),
            dma((units * (p.comp - 1),)),
            dma((units * (p.comp - 1),)),
            dma((units * p.stages,)),
            dma((units * p.stages,)),
            dma((swap_count * len(p.swap_peers),)),
            dma((swap_count * len(p.swap_peers),)),
            dma((2 * swap_count,)),
            dma((2 * swap_count,)),
            dma(((p.comp - 1) * OUT_PIECES,)),
            dma(((p.comp - 1) * OUT_PIECES,)),
        ],
        compiler_params=pltpu.CompilerParams(
            collective_id=0, has_side_effects=True, vmem_limit_bytes=LIMIT
        ),
    )(
        angle, raw, filt, weights, offsets, delay, jnp.asarray(constants.T), jnp.asarray(constants.T),
        jnp.asarray(twiddle(radix)),
    )


def body(raw_pulses, range_filter, steer_angle, band_offsets, band_weights, beam_delay):
    counts = (lax.axis_size("sub"), lax.axis_size("beam"), lax.axis_size("comp"))
    columns = band_offsets.shape[1]
    plan = Plan(counts, steer_angle.shape, raw_pulses.shape[2], columns)
    radix = plan.radix
    filt = range_filter.reshape(2, radix, radix).transpose(1, 0, 2).reshape(2 * radix, radix)
    out = fused(
        plan, steer_angle, raw_pulses, filt, band_weights.transpose(0, 2, 1), band_offsets, beam_delay
    )
    out = store(out)
    out = out.reshape(plan.outs, plan.quarter, 2, radix).transpose(0, 2, 1, 3)
    return out.reshape(plan.outs, 2, plan.quarter * radix)


def solution(mesh):
    in_specs = (
        P(("sub", "beam", "comp"), None, None),
        P(),
        P(None, ("sub", "beam", "comp")),
        P(None, ("beam", "comp")),
        P(None, ("beam", "comp"), None),
        P(None, ("beam", "comp")),
    )
    out_specs = P(("beam", "comp"), None, "sub")
    return jax.shard_map(body, mesh=mesh, in_specs=in_specs, out_specs=out_specs, check_vma=False)
```

```python
import functools
import itertools
import math

import jax
import jax.numpy as jnp
import numpy as np
from jax import lax
from jax.experimental import pallas as pl
from jax.experimental.pallas import tpu as pltpu
from jax.sharding import PartitionSpec as P

BAND = 8
EXTRA = 8
SIDE = 12
GROUP = 2
PIECES = 4
LAG = 3
LAG_TWO = 2
LAST_PIECES = 4
BEAM_FIRST = (1, 4, 7, 11)
OUT_PIECES = 4
HALO_LAG = 2
LIMIT = 54 * 2**20
STORES = 4
MESH = pl.DeviceIdType.MESH
F32 = jnp.float32
BF16 = jnp.bfloat16


def dft_table(length):
    index_row = np.arange(length, dtype=np.int32)
    product = index_row[:, None] * index_row[None, :] % length
    phase_angle = product.astype(np.float32) * np.float32(2.0 * math.pi / length)
    return np.cos(phase_angle).astype(BF16), (-np.sin(phase_angle)).astype(BF16)


def real_form(length):
    cos_part, sin_part = dft_table(length)
    upper_rows = np.concatenate([cos_part, sin_part], axis=1)
    lower_rows = np.concatenate([-sin_part, cos_part], axis=1)
    return np.concatenate([upper_rows, lower_rows], axis=0)


def twiddle(radix):
    index_row = np.arange(radix, dtype=np.int32)
    product = index_row[:, None] * index_row[None, :] % (radix * radix)
    phase_angle = product.astype(np.float32) * np.float32(2.0 * math.pi / (radix * radix))
    return np.stack([np.cos(phase_angle), -np.sin(phase_angle)], 0).astype(np.float32)


def split(value):
    high = value.astype(BF16)
    return high, (value - high.astype(F32)).astype(BF16)


def dot(a, b):
    return jnp.dot(a, b, preferred_element_type=F32)


class Plan:
    def __init__(self, counts, angle_shape, length, columns):
        self.sub, self.beam, self.comp = counts
        self.blocks = self.beam * self.comp
        self.beams, self.pulses = angle_shape
        self.first = self.beams // self.blocks
        self.length = length
        self.radix = math.isqrt(length)
        self.columns = columns
        self.group = min(GROUP, self.first)
        self.groups = self.first // self.group
        self.rows = 2 * self.group
        self.counts = [PIECES] * (self.groups - 1) + [LAST_PIECES]
        self.units = [(g, h) for g in range(self.groups) for h in range(self.counts[g])]
        self.beam_first = [self.units[i] for i in BEAM_FIRST]
        self.levels = self.sub.bit_length() - 1
        self.quarter = self.radix // self.sub
        self.share = self.quarter // self.comp
        self.outs = self.first * self.sub
        self.padded = -(-columns // 128) * 128
        self.stages = self.beam.bit_length() - 1
        self.slots = self.comp + 2
        self.factor = float(self.pulses * self.blocks) ** (-0.5)
        self.sizes = []
        for level in range(self.levels):
            own = self.comp * self.first * 2 ** (level + 1)
            self.sizes.append(own + (0 if level == self.levels - 1 else 2 * EXTRA))
        self.depths = [2 * self.slots * self.first] + [2 * n for n in self.sizes[:-1]]
        near = {(0, d, e) for d in (-1, 0, 1) for e in range(self.comp)}
        near |= {(d, 0, e) for d in range(self.sub) for e in range(self.comp)}
        near |= {(0, d, 0) for d in range(self.beam)}
        self.peers = sorted({(d % self.sub, e % self.beam, f % self.comp) for d, e, f in near} - {(0, 0, 0)})
        need = BAND // 2
        for _ in range(self.levels - 1):
            need = (need + 1) // 2 + BAND // 2
        need = min(need, self.first) if self.comp > 1 else self.first
        self.edges = [g for g in range(self.groups) if g * self.group < need]
        self.swap_peers = [
            (d, e) for d in range(self.sub) for e in range(self.comp) if (d, e) != (0, 0)
        ]

    def pieces(self, level):
        new = self.first * 2 ** (level + 1)
        inner = [(k, 0, new) for k in range(self.comp)]
        if level == self.levels - 1:
            return inner
        return [(-1, new - EXTRA, EXTRA)] + inner + [(self.comp, 0, EXTRA)]


def fused_kernel(
    plan, angle_hbm, raw_hbm, filter_hbm, weights_hbm, offsets_hbm, delay_hbm, first_hbm,
    second_hbm, turn_hbm, out_ref, angle_ref, weights_ref, offsets_ref, delay_ref, raw, weight, part, recv_one, swap, first, second, turn, filt,
    blend, image, window, mine, tables, fields, *rest,
):
    p = plan
    levels = p.levels
    rest = list(rest)

    def take(number):
        taken = rest[:number]
        del rest[:number]
        return taken

    held, recv_two = take(p.stages), take(p.stages)
    wide_held, wide_recv = take(p.stages), take(p.stages)
    late_held, late_recv = take(2)
    lhs, delay, phase = take(levels), take(levels), take(levels)
    (final, outbound, inbound, load_sem, const_sem, table_send, table_recv, one_send, one_recv,
     two_send, two_recv, swap_send, swap_recv, halo_send, halo_recv, out_send, out_recv) = rest
    s = lax.axis_index("sub")
    b = lax.axis_index("beam")
    c = lax.axis_index("comp")
    has_low = b > 0
    has_high = b < p.beam - 1
    radix = p.radix

    def at(ds, db, dc):
        return {
            "sub": lax.rem(s + (ds % p.sub), p.sub),
            "beam": lax.rem(b + (db % p.beam), p.beam),
            "comp": lax.rem(c + (dc % p.comp), p.comp),
        }

    def remote(source, target, send, recv, place):
        return pltpu.make_async_remote_copy(
            src_ref=source, dst_ref=target, send_sem=send, recv_sem=recv, device_id=place,
            device_id_type=MESH,
        )

    angle_load = pltpu.make_async_copy(angle_hbm, angle_ref, const_sem.at[7])
    angle_load.start()
    def columns_of(g, h):
        width = p.length // p.counts[g]
        return pl.ds(h * width, width)

    loads = []
    for h in range(PIECES):
        cols = columns_of(0, h)
        loads.append(
            pltpu.make_async_copy(raw_hbm.at[:, :, cols], raw.at[:, :, cols], load_sem.at[h])
        )
        loads[h].start()
    constants = [
        pltpu.make_async_copy(source, target, const_sem.at[i])
        for i, (source, target) in enumerate(
            [
                (weights_hbm, weights_ref), (offsets_hbm, offsets_ref), (delay_hbm, delay_ref),
                (first_hbm, first), (second_hbm, second), (turn_hbm, turn), (filter_hbm, filt),
            ]
        )
    ]
    for copy in constants:
        copy.start()

    window[:, 0] = jnp.zeros(window.shape[:1] + window.shape[2:], BF16)
    window[:, p.comp + 1] = jnp.zeros(window.shape[:1] + window.shape[2:], BF16)
    barrier = pltpu.get_barrier_semaphore()
    for place in p.peers:
        pl.semaphore_signal(barrier, inc=1, device_id=at(*place), device_id_type=MESH)

    angle_load.wait()
    angle = angle_ref[...]
    cos_part = (jnp.cos(angle) * p.factor).astype(BF16)
    sin_part = (jnp.sin(angle) * p.factor).astype(BF16)
    stacked = jnp.concatenate(
        [
            jnp.concatenate([cos_part, -sin_part], axis=1),
            jnp.concatenate([sin_part, cos_part], axis=1),
        ],
        axis=0,
    )
    count, deep = 2 * p.beams, 2 * p.pulses
    source = lax.broadcasted_iota(jnp.int32, (deep, deep), 0)
    target = lax.broadcasted_iota(jnp.int32, (deep, deep), 1)
    place = jnp.where(source < p.pulses, 2 * source, 2 * (source - p.pulses) + 1)
    spread = jnp.where(place == target, 1.0, 0.0).astype(BF16)
    target = lax.broadcasted_iota(jnp.int32, (count, count), 0)
    source = lax.broadcasted_iota(jnp.int32, (count, count), 1)

    def bits(value, size):
        return jnp.bitwise_and(value, size - 1), lax.shift_right_logical(
            value, jnp.full_like(value, size.bit_length() - 1)
        )

    def order_of(group_at, comp_at):
        return jnp.where(comp_at == p.comp - 1, p.groups - 1 - group_at, group_at)

    within, upper = bits(target, p.group)
    half, upper = bits(upper, 2)
    beam_at, upper = bits(upper, p.beam)
    comp_at, group_at = bits(upper, p.comp)
    group_at = order_of(group_at, comp_at)
    origin = half * p.beams + (
        (beam_at * p.comp + comp_at) * p.first + group_at * p.group + within
    )
    order = jnp.where(origin == source, 1.0, 0.0).astype(BF16)
    weight[...] = dot(order, dot(stacked, spread).astype(BF16)).astype(BF16)

    def table_copy(db, dc):
        slot = 1 + c if db == 0 else (0 if db > 0 else p.comp + 1)
        k = (db + 1) * p.comp + dc
        r = dc if db == 0 else (0 if db > 0 else p.comp)
        return remote(mine, tables.at[slot], table_send.at[k], table_recv.at[r], at(0, db, dc))

    def table_ends(action):
        @pl.when(c == p.comp - 1)
        def _():
            for e in range(p.comp):
                action(table_copy(1, e))

        @pl.when(c == 0)
        def _():
            for e in range(p.comp):
                action(table_copy(-1, e))

    def send_tables():
        for copy in constants[:3]:
            copy.wait()
        mine[...] = jnp.zeros(mine.shape, F32)
        for side in range(2):
            row = side * SIDE
            mine[row : row + BAND, : p.columns] = weights_ref[side]
            mine[row + BAND : row + BAND + 1, : p.columns] = offsets_ref[side : side + 1].astype(F32)
            mine[row + BAND + 1 : row + BAND + 2, : p.columns] = delay_ref[side : side + 1]
        tables[1 + c] = mine[...]
        for e in range(1, p.comp):
            table_copy(0, e).start()
        table_ends(lambda copy: copy.start())

    one, two, swaps = {}, {}, {}

    def bit(stage):
        return lax.rem(lax.div(b, 2**stage), 2)

    def form(h):
        loads[h].wait()
        cols = columns_of(0, h)
        pulses = raw[:, :, cols].reshape(2 * p.pulses, -1)
        product = dot(weight[...], pulses).astype(BF16)
        part[:, :, :, :, :, cols] = product.reshape(
            p.groups, p.comp, p.beam // 2, 2, p.rows, -1
        )

    def partner(stage):
        return {"beam": b + (1 - 2 * bit(stage)) * 2**stage}

    def start_one(g, h):
        if (g, h) in p.beam_first:
            n = p.beam_first.index((g, h))
            return send_wide(0, n, part.at[g, :, :, 1 - bit(0), :, columns_of(g, h)])
        one[g, h] = []
        for d in range(1, p.comp):
            peer = lax.rem(c + d, p.comp)
            k = p.units.index((g, h)) * (p.comp - 1) + d - 1
            copy = remote(
                part.at[g, peer, :, :, :, columns_of(g, h)],
                recv_one.at[d - 1, g, :, :, :, columns_of(g, h)],
                one_send.at[k], one_recv.at[k], at(0, 0, d),
            )
            copy.start()
            one[g, h].append(copy)

    def send_wide(stage, n, source):
        k = p.units.index(p.beam_first[n]) * p.stages + stage
        copy = remote(
            source, wide_recv[stage].at[n], two_send.at[k], two_recv.at[k], partner(stage)
        )
        copy.start()
        two[(stage,) + p.beam_first[n]] = copy

    def gathered_wide(stage, n):
        g, h = p.beam_first[n]
        two[stage, g, h].wait_recv()
        if stage == 0:
            total = part[g, :, :, bit(0), :, columns_of(g, h)].astype(F32)
        else:
            total = wide_held[stage][n, :, :, bit(stage)].astype(F32)
        return total + wide_recv[stage][n].astype(F32)

    def step_wide(stage, n):
        total = gathered_wide(stage - 1, n)
        if stage < p.stages:
            wide_held[stage][n] = total.astype(BF16).reshape(wide_held[stage].shape[1:])
            return send_wide(stage, n, wide_held[stage].at[n, :, :, 1 - bit(stage)])
        g, h = p.beam_first[n]
        late_held[n] = total[:, 0].astype(BF16)
        one[g, h] = []
        for d in range(1, p.comp):
            k = p.units.index((g, h)) * (p.comp - 1) + d - 1
            copy = remote(
                late_held.at[n, lax.rem(c + d, p.comp)], late_recv.at[n, d - 1],
                one_send.at[k], one_recv.at[k], at(0, 0, d),
            )
            copy.start()
            one[g, h].append(copy)

    def send_two(stage, g, h, total):
        cols = columns_of(g, h)
        held[stage][g, :, :, :, cols] = total.astype(BF16).reshape(-1, 2, p.rows, cols.size)
        k = p.units.index((g, h)) * p.stages + stage
        copy = remote(
            held[stage].at[g, :, 1 - bit(stage), :, cols],
            recv_two[stage].at[g, :, :, cols],
            two_send.at[k], two_recv.at[k], partner(stage),
        )
        copy.start()
        two[stage, g, h] = copy

    def gathered(stage, g, h):
        cols = columns_of(g, h)
        two[stage, g, h].wait_recv()
        total = held[stage][g, :, bit(stage), :, cols].astype(F32)
        return total + recv_two[stage][g, :, :, cols].astype(F32)

    def step_beam(stage, g, h):
        if (g, h) in p.beam_first:
            return step_wide(stage + 1, p.beam_first.index((g, h)))
        if stage > 0:
            return send_two(stage, g, h, gathered(stage - 1, g, h))
        cols = columns_of(g, h)
        for copy in one[g, h]:
            copy.wait_recv()
        total = part[g, c, :, :, :, cols].astype(F32)
        for d in range(1, p.comp):
            total += recv_one[d - 1, g, :, :, :, cols].astype(F32)
        send_two(0, g, h, total)

    def finish(g, h):
        if (g, h) in p.beam_first:
            n = p.beam_first.index((g, h))
            total = late_held[n, c].astype(F32)
            for copy in one[g, h]:
                copy.wait_recv()
            for d in range(1, p.comp):
                total += late_recv[n, d - 1].astype(F32)
        else:
            total = gathered(p.stages - 1, g, h)[0]
        width = p.length // p.counts[g]
        for a in range(width // radix):
            swap[pl.ds(h * (width // radix) + a, p.rows, stride=radix), :] = total[
                :, a * radix : (a + 1) * radix
            ]

    deferred = []

    def compress(g, deferring):
        factor = p.length ** (-0.5)
        h_real = filt[pl.ds(0, radix, stride=2), :] * factor
        h_imag = filt[pl.ds(1, radix, stride=2), :] * factor
        span = p.group * radix

        @pl.loop(0, p.group // 2)
        def _(pair):
            sides = []
            for u in range(2):
                row = pl.multiple_of((2 * pair + u) * radix, radix)
                sides.append(
                    jnp.concatenate(
                        [swap[pl.ds(row, radix), :], swap[pl.ds(row + span, radix), :]], axis=0
                    )
                )
            high, low = split(jnp.concatenate(sides, axis=1))
            section = dot(first[...], high) + dot(first[...], low)
            cos_turn, sin_turn = turn[0], turn[1]
            turned = []
            for u in range(2):
                real = section[:radix, u * radix : (u + 1) * radix]
                imag = section[radix:, u * radix : (u + 1) * radix]
                turned.append(
                    jnp.concatenate(
                        [
                            real * cos_turn - imag * sin_turn,
                            real * sin_turn + imag * cos_turn,
                        ],
                        axis=1,
                    )
                )
            high, low = split(jnp.concatenate(turned, axis=0))
            both_last = (((1,), (1,)), ((), ()))
            spectrum = lax.dot_general(second[...], high, both_last, preferred_element_type=F32)
            spectrum += lax.dot_general(second[...], low, both_last, preferred_element_type=F32)
            for u in range(2):
                real = spectrum[:radix, u * radix : (u + 1) * radix]
                imag = spectrum[radix:, u * radix : (u + 1) * radix]
                row = 2 * pair + u
                blend[pl.ds(row, radix, stride=p.rows), :] = real * h_real - imag * h_imag
                blend[pl.ds(row + p.group, radix, stride=p.rows), :] = (
                    real * h_imag + imag * h_real
                )

        image[g] = blend[...].reshape(radix, p.rows, radix).astype(BF16)
        window[s, 1 + c, g] = image[g, pl.ds((s * p.comp + c) * p.share, p.share)]
        number = OUT_PIECES if g == p.groups - 1 else 1
        size = p.share // number
        for o in range(number):
            swaps[g, o] = []
            for i, (ds, dc) in enumerate(p.swap_peers):
                where = at(ds, 0, dc)
                begin = (where["sub"] * p.comp + where["comp"]) * p.share + o * size
                k = (g + o) * len(p.swap_peers) + i
                copy = remote(
                    image.at[g, pl.ds(begin, size)],
                    window.at[s, 1 + c, g, pl.ds(o * size, size)],
                    swap_send.at[k], swap_recv.at[k], where,
                )
                swaps[g, o].append(copy)
                if dc == 0 or not deferring:
                    copy.start()
                else:
                    deferred.append(copy)

    def halo_copy(g, o, step):
        near, far = (1, p.comp + 1) if step < 0 else (p.comp, 0)
        size = p.share // (OUT_PIECES if g == p.groups - 1 else 1)
        k = 2 * (g + o) + (0 if step < 0 else 1)
        return remote(
            window.at[:, near, g, pl.ds(o * size, size)],
            window.at[:, far, g, pl.ds(o * size, size)],
            halo_send.at[k], halo_recv.at[k], {"beam": b + step},
        )

    def start_halo(g, o=0):
        for copy in swaps[g, o]:
            copy.wait_recv()
        if g not in p.edges:
            return

        @pl.when(has_low)
        def _():
            halo_copy(g, o, -1).start()

        @pl.when(has_high)
        def _():
            halo_copy(g, o, 1).start()

    def wait_halo(g, o=0):
        if g not in p.edges:
            return

        @pl.when(has_low)
        def _():
            halo_copy(g, o, 1).wait_recv()
            halo_copy(g, o, -1).wait_send()

        @pl.when(has_high)
        def _():
            halo_copy(g, o, -1).wait_recv()
            halo_copy(g, o, 1).wait_send()

    def read_tables():
        for e in range(1, p.comp):
            table_copy(0, e).wait_recv()
        table_copy(1, 0).wait_recv()
        table_copy(-1, 0).wait_recv()
        for j in range(p.padded // 128):
            block = tables[:, :, j * 128 : (j + 1) * 128].reshape(-1, 128)
            short = 128 - block.shape[0]
            if short > 0:
                block = jnp.concatenate([block, jnp.zeros((short, 128), F32)], axis=0)
            fields[j * 128 : (j + 1) * 128, :] = block.T

    def fields_of(level, side):
        for step, begin, size in p.pieces(level):
            row = p.first * (2 ** (level + 1) - 2) + begin
            yield step, size, row, (step + 1) * 2 * SIDE + side * SIDE

    def build(level):
        depth, size = p.depths[level], p.sizes[level]
        child = p.first * 2**level
        lane = lax.broadcasted_iota(jnp.int32, (1, depth), 1)
        if level == 0:
            within, upper = bits(lane, p.group)
            half, upper = bits(upper, 2)
            group_at, slot = bits(upper, p.groups)
            comp_at = jnp.where(slot == 0, p.comp - 1, jnp.where(slot > p.comp, 0, slot - 1))
            group_at = order_of(group_at, comp_at)
            beam_at = slot * p.first + group_at * p.group + within
        else:
            half = jnp.where(lane < depth // 2, 0, 1)
            beam_at = lane - half * (depth // 2)
        begin = p.first if level == 0 else EXTRA
        for side in range(2):
            done = 0
            for step, rows, row, base in fields_of(level, side):
                block = fields[row : row + rows, base : base + SIDE]
                shift = block[:, BAND : BAND + 1].astype(jnp.int32)
                tap = beam_at - begin - step * child - shift
                band = jnp.zeros((rows, depth), F32)
                for t in range(BAND):
                    band += jnp.where(tap == t, block[:, t : t + 1], 0.0)
                if step < 0:
                    band = jnp.where(has_low, band, 0.0)
                if step >= p.comp:
                    band = jnp.where(has_high, band, 0.0)
                for r in range(2):
                    high, low = split(jnp.where(half == r, band, 0.0))
                    lhs[level][side, 0, r * size + done : r * size + done + rows, :] = high
                    lhs[level][side, 1, r * size + done : r * size + done + rows, :] = low
                delay[level][side, done : done + rows, :] = jnp.broadcast_to(
                    block[:, BAND + 1 : BAND + 2], (rows, radix)
                )
                done += rows

    def build_phases(begin, end):
        start = (s * p.comp + c) * p.share

        @pl.loop(begin, end)
        def _(m):
            for level in range(levels):
                for side in range(2):
                    factor = delay[level][side]
                    lane = lax.broadcasted_iota(jnp.int32, factor.shape, 1)
                    place = ((start + m) * radix + lane).astype(F32)
                    phase_angle = factor * (1.0 + place / p.length)
                    phase[level][0, side, m] = jnp.cos(phase_angle)
                    phase[level][1, side, m] = jnp.sin(phase_angle)

    def merge(m):
        def pair(load):
            return jnp.concatenate([load(m), load(m + 1)], axis=1)

        images = [
            pair(lambda k, i=i: window[i, :, :, k].reshape(p.depths[0], radix))
            for i in range(p.sub)
        ]
        for level in range(levels):
            size = p.sizes[level]
            merged = []
            for g in range(len(images) // 2):
                real, imag = 0.0, 0.0
                for side in range(2):
                    child = images[2 * g + side]
                    mixed = dot(lhs[level][side, 0], child) + dot(lhs[level][side, 1], child)
                    cosine = pair(lambda k: phase[level][0, side, k])
                    sine = pair(lambda k: phase[level][1, side, k])
                    real += cosine * mixed[:size] - sine * mixed[size:]
                    imag += sine * mixed[:size] + cosine * mixed[size:]
                merged.append((real, imag))
            if level + 1 < levels:
                images = [jnp.concatenate(parts, axis=0).astype(BF16) for parts in merged]
        for r in range(2):
            for k in range(p.comp):
                for u in range(2):
                    value = merged[0][r][k * p.outs : (k + 1) * p.outs, u * radix : (u + 1) * radix]
                    final[k, m + u, r * p.outs : (r + 1) * p.outs, :] = value
                    outbound[k, m + u, r * p.outs : (r + 1) * p.outs, :] = value.astype(BF16)

    def place_out(source, m, column):
        for r in range(2):
            value = source[r * p.outs : (r + 1) * p.outs].astype(F32)
            out_ref[pl.ds(2 * (column * p.share + m) + r, p.outs, stride=2 * p.quarter), :] = value

    units = p.units
    total_units = len(units)
    idle = range(PIECES, 2 * PIECES)
    per_step = -(-p.share // len(idle))
    pending = []
    last = p.groups - 1
    drain = LAG + LAG_TWO * p.stages
    form(0)
    pl.semaphore_wait(barrier, len(p.peers))
    for u in range(total_units + drain):
        if 0 < u < PIECES:
            form(u)
        if u < total_units:
            start_one(*units[u])
        if u == 1:
            send_tables()
        if u == total_units - 1:
            for copy in deferred:
                copy.start()
        for stage in range(p.stages):
            v = u - LAG - LAG_TWO * stage
            if 0 <= v < total_units:
                step_beam(stage, *units[v])
        v = u - drain
        while pending and v >= pending[0][0]:
            start_halo(pending.pop(0)[1])
        if u == PIECES:
            read_tables()
            for copy in constants[3:]:
                copy.wait()
            for level in range(levels):
                build(level)
        if u in idle:
            begin = min((u - PIECES) * per_step, p.share)
            end = min(begin + per_step, p.share)
            if end > begin:
                build_phases(begin, end)
        if v >= 0:
            finish(*units[v])
            g, h = units[v]
            if h == p.counts[g] - 1:
                compress(g, u < total_units - 1)
                if g < last:
                    pending.append((max(v + HALO_LAG, total_units - drain + 4), g))
    for _, g in pending:
        start_halo(g)
    for g in range(last):
        wait_halo(g)

    chunk = p.share // OUT_PIECES
    outs = []

    def merge_piece(o):
        @pl.loop(0, chunk // 2)
        def _(i):
            merge(o * chunk + 2 * i)

        for d in range(1, p.comp):
            peer = lax.rem(c + d, p.comp)
            k = (d - 1) * OUT_PIECES + o
            copy = remote(
                outbound.at[peer, pl.ds(o * chunk, chunk)],
                inbound.at[d - 1, pl.ds(o * chunk, chunk)],
                out_send.at[k], out_recv.at[k], at(0, 0, d),
            )
            copy.start()
            outs.append((o, d, copy))

    for o in range(OUT_PIECES):
        start_halo(last, o)
        if last not in p.edges:
            merge_piece(o)
    if last in p.edges:
        for o in range(OUT_PIECES):
            wait_halo(last, o)
            merge_piece(o)

    @pl.loop(0, p.share)
    def _(m):
        place_out(final[c, m], m, c)

    for o, d, copy in outs:
        copy.wait_recv()
        origin = lax.rem(c + p.comp - d, p.comp)

        @pl.loop(0, chunk)
        def _(i, o=o, d=d, origin=origin):
            place_out(inbound[d - 1, o * chunk + i], o * chunk + i, origin)

    for e in range(1, p.comp):
        table_copy(0, e).wait_send()
    table_ends(lambda copy: copy.wait_send())
    for copy in itertools.chain(
        *one.values(), two.values(), *swaps.values(), (entry[2] for entry in outs)
    ):
        copy.wait_send()


def store_kernel(value_ref, out_hbm, sem):
    size = value_ref.shape[0] // STORES
    copies = [
        pltpu.make_async_copy(
            value_ref.at[pl.ds(i * size, size)], out_hbm.at[pl.ds(i * size, size)], sem.at[i]
        )
        for i in range(STORES)
    ]
    for copy in copies:
        copy.start()
    for copy in copies:
        copy.wait()


def store(value):
    return pl.pallas_call(
        store_kernel,
        out_shape=jax.ShapeDtypeStruct(value.shape, value.dtype),
        in_specs=[pl.BlockSpec(memory_space=pltpu.VMEM)],
        out_specs=pl.BlockSpec(memory_space=pl.ANY),
        scratch_shapes=[pltpu.SemaphoreType.DMA((STORES,))],
        compiler_params=pltpu.CompilerParams(vmem_limit_bytes=8 * 2**20),
    )(value)


def fused(plan, angle, raw, filt, weights, offsets, delay):
    p = plan
    constants = real_form(p.radix)
    dma = pltpu.SemaphoreType.DMA
    radix = p.radix
    units = len(p.units)
    wide = p.length // PIECES
    early = len(p.beam_first)
    halves = [p.beam // 2 ** (t + 1) for t in range(p.stages)]
    swap_count = p.groups - 1 + OUT_PIECES
    return pl.pallas_call(
        functools.partial(fused_kernel, p),
        out_shape=pltpu.VMEM((p.outs * 2 * p.quarter, radix), F32),
        in_specs=[pl.BlockSpec(memory_space=pltpu.HBM)] * 9,
        out_specs=pl.BlockSpec(memory_space=pltpu.VMEM),
        scratch_shapes=[
            pltpu.VMEM(angle.shape, F32),
            pltpu.VMEM(weights.shape, F32),
            pltpu.VMEM(offsets.shape, jnp.int32),
            pltpu.VMEM(delay.shape, F32),
            pltpu.VMEM(raw.shape, BF16),
            pltpu.VMEM((2 * p.beams, 2 * p.pulses), BF16),
            pltpu.VMEM((p.groups, p.comp, p.beam // 2, 2, p.rows, p.length), BF16),
            pltpu.VMEM((p.comp - 1, p.groups, p.beam // 2, 2, p.rows, p.length), BF16),
            pltpu.VMEM((p.rows * radix, radix), F32),
            pltpu.VMEM((2 * radix, 2 * radix), BF16),
            pltpu.VMEM((2 * radix, 2 * radix), BF16),
            pltpu.VMEM((2, radix, radix), F32),
            pltpu.VMEM((2 * radix, radix), F32),
            pltpu.VMEM((p.rows * radix, radix), F32),
            pltpu.VMEM((p.groups, radix, p.rows, radix), BF16),
            pltpu.VMEM((p.sub, p.slots, p.groups, p.share, p.rows, radix), BF16),
            pltpu.VMEM((2 * SIDE, p.padded), F32),
            pltpu.VMEM((p.slots, 2 * SIDE, p.padded), F32),
            pltpu.VMEM((p.padded, 128), F32),
            *[pltpu.VMEM((p.groups, n, 2, p.rows, p.length), BF16) for n in halves],
            *[pltpu.VMEM((p.groups, n, p.rows, p.length), BF16) for n in halves],
            *[
                pltpu.VMEM((early, p.comp, n if t else 1, 2, p.rows, wide if t else 128), BF16)
                for t, n in enumerate(halves)
            ],
            *[pltpu.VMEM((early, p.comp, n, p.rows, wide), BF16) for n in halves],
            pltpu.VMEM((early, p.comp, p.rows, wide), BF16),
            pltpu.VMEM((early, p.comp - 1, p.rows, wide), BF16),
            *[pltpu.VMEM((2, 2, 2 * n, k), BF16) for n, k in zip(p.sizes, p.depths)],
            *[pltpu.VMEM((2, n, radix), F32) for n in p.sizes],
            *[pltpu.VMEM((2, 2, p.share, n, radix), F32) for n in p.sizes],
            pltpu.VMEM((p.comp, p.share, 2 * p.outs, radix), F32),
            pltpu.VMEM((p.comp, p.share, 2 * p.outs, radix), BF16),
            pltpu.VMEM((p.comp - 1, p.share, 2 * p.outs, radix), BF16),
            dma((PIECES,)),
            dma((8,)),
            dma((3 * p.comp,)),
            dma((p.comp + 1,)),
            dma((units * (p.comp - 1),)),
            dma((units * (p.comp - 1),)),
            dma((units * p.stages,)),
            dma((units * p.stages,)),
            dma((swap_count * len(p.swap_peers),)),
            dma((swap_count * len(p.swap_peers),)),
            dma((2 * swap_count,)),
            dma((2 * swap_count,)),
            dma(((p.comp - 1) * OUT_PIECES,)),
            dma(((p.comp - 1) * OUT_PIECES,)),
        ],
        compiler_params=pltpu.CompilerParams(
            collective_id=0, has_side_effects=True, vmem_limit_bytes=LIMIT
        ),
    )(
        angle, raw, filt, weights, offsets, delay, jnp.asarray(constants.T), jnp.asarray(constants.T),
        jnp.asarray(twiddle(radix)),
    )


def body(raw_pulses, range_filter, steer_angle, band_offsets, band_weights, beam_delay):
    counts = (lax.axis_size("sub"), lax.axis_size("beam"), lax.axis_size("comp"))
    columns = band_offsets.shape[1]
    plan = Plan(counts, steer_angle.shape, raw_pulses.shape[2], columns)
    radix = plan.radix
    filt = range_filter.reshape(2, radix, radix).transpose(1, 0, 2).reshape(2 * radix, radix)
    out = fused(
        plan, steer_angle, raw_pulses, filt, band_weights.transpose(0, 2, 1), band_offsets, beam_delay
    )
    out = store(out)
    out = out.reshape(plan.outs, plan.quarter, 2, radix).transpose(0, 2, 1, 3)
    return out.reshape(plan.outs, 2, plan.quarter * radix)


def solution(mesh):
    in_specs = (
        P(("sub", "beam", "comp"), None, None),
        P(),
        P(None, ("sub", "beam", "comp")),
        P(None, ("beam", "comp")),
        P(None, ("beam", "comp"), None),
        P(None, ("beam", "comp")),
    )
    out_specs = P(("beam", "comp"), None, "sub")
    return jax.shard_map(body, mesh=mesh, in_specs=in_specs, out_specs=out_specs, check_vma=False)
```

```python
import functools
import itertools
import math

import jax
import jax.numpy as jnp
import numpy as np
from jax import lax
from jax.experimental import pallas as pl
from jax.experimental.pallas import tpu as pltpu
from jax.sharding import PartitionSpec as P

BAND = 8
EXTRA = 8
SIDE = 12
GROUP = 2
PIECES = 4
LAG = 3
LAG_TWO = 2
LAST_PIECES = 4
BEAM_FIRST = (1, 4, 7, 11)
OUT_PIECES = 4
HALO_LAG = 1
LIMIT = 54 * 2**20
STORES = 4
MESH = pl.DeviceIdType.MESH
F32 = jnp.float32
BF16 = jnp.bfloat16


def dft_table(length):
    index_row = np.arange(length, dtype=np.int32)
    product = index_row[:, None] * index_row[None, :] % length
    phase_angle = product.astype(np.float32) * np.float32(2.0 * math.pi / length)
    return np.cos(phase_angle).astype(BF16), (-np.sin(phase_angle)).astype(BF16)


def real_form(length):
    cos_part, sin_part = dft_table(length)
    upper_rows = np.concatenate([cos_part, sin_part], axis=1)
    lower_rows = np.concatenate([-sin_part, cos_part], axis=1)
    return np.concatenate([upper_rows, lower_rows], axis=0)


def twiddle(radix):
    index_row = np.arange(radix, dtype=np.int32)
    product = index_row[:, None] * index_row[None, :] % (radix * radix)
    phase_angle = product.astype(np.float32) * np.float32(2.0 * math.pi / (radix * radix))
    return np.stack([np.cos(phase_angle), -np.sin(phase_angle)], 0).astype(np.float32)


def split(value):
    high = value.astype(BF16)
    return high, (value - high.astype(F32)).astype(BF16)


def dot(a, b):
    return jnp.dot(a, b, preferred_element_type=F32)


class Plan:
    def __init__(self, counts, angle_shape, length, columns):
        self.sub, self.beam, self.comp = counts
        self.blocks = self.beam * self.comp
        self.beams, self.pulses = angle_shape
        self.first = self.beams // self.blocks
        self.length = length
        self.radix = math.isqrt(length)
        self.columns = columns
        self.group = min(GROUP, self.first)
        self.groups = self.first // self.group
        self.rows = 2 * self.group
        self.counts = [PIECES] * (self.groups - 1) + [LAST_PIECES]
        self.units = [(g, h) for g in range(self.groups) for h in range(self.counts[g])]
        self.beam_first = [self.units[i] for i in BEAM_FIRST]
        self.levels = self.sub.bit_length() - 1
        self.quarter = self.radix // self.sub
        self.share = self.quarter // self.comp
        self.outs = self.first * self.sub
        self.padded = -(-columns // 128) * 128
        self.stages = self.beam.bit_length() - 1
        self.slots = self.comp + 2
        self.factor = float(self.pulses * self.blocks) ** (-0.5)
        self.sizes = []
        for level in range(self.levels):
            own = self.comp * self.first * 2 ** (level + 1)
            self.sizes.append(own + (0 if level == self.levels - 1 else 2 * EXTRA))
        self.depths = [2 * self.slots * self.first] + [2 * n for n in self.sizes[:-1]]
        near = {(0, d, e) for d in (-1, 0, 1) for e in range(self.comp)}
        near |= {(d, 0, e) for d in range(self.sub) for e in range(self.comp)}
        near |= {(0, d, 0) for d in range(self.beam)}
        self.peers = sorted({(d % self.sub, e % self.beam, f % self.comp) for d, e, f in near} - {(0, 0, 0)})
        need = BAND // 2
        for _ in range(self.levels - 1):
            need = (need + 1) // 2 + BAND // 2
        need = min(need, self.first) if self.comp > 1 else self.first
        self.edges = [g for g in range(self.groups) if g * self.group < need]
        self.swap_peers = [
            (d, e)
            for d in reversed(range(self.sub))
            for e in reversed(range(self.comp))
            if (d, e) != (0, 0)
        ]

    def pieces(self, level):
        new = self.first * 2 ** (level + 1)
        inner = [(k, 0, new) for k in range(self.comp)]
        if level == self.levels - 1:
            return inner
        return [(-1, new - EXTRA, EXTRA)] + inner + [(self.comp, 0, EXTRA)]


def fused_kernel(
    plan, angle_hbm, raw_hbm, filter_hbm, weights_hbm, offsets_hbm, delay_hbm, first_hbm,
    second_hbm, turn_hbm, out_ref, angle_ref, weights_ref, offsets_ref, delay_ref, raw, weight, part, recv_one, swap, first, second, turn, filt,
    blend, image, window, mine, tables, fields, *rest,
):
    p = plan
    levels = p.levels
    rest = list(rest)

    def take(number):
        taken = rest[:number]
        del rest[:number]
        return taken

    held, recv_two = take(p.stages), take(p.stages)
    wide_held, wide_recv = take(p.stages), take(p.stages)
    late_held, late_recv = take(2)
    lhs, delay, phase = take(levels), take(levels), take(levels)
    (final, outbound, inbound, load_sem, const_sem, table_send, table_recv, one_send, one_recv,
     two_send, two_recv, swap_send, swap_recv, halo_send, halo_recv, out_send, out_recv) = rest
    s = lax.axis_index("sub")
    b = lax.axis_index("beam")
    c = lax.axis_index("comp")
    has_low = b > 0
    has_high = b < p.beam - 1
    radix = p.radix

    def at(ds, db, dc):
        return {
            "sub": lax.rem(s + (ds % p.sub), p.sub),
            "beam": lax.rem(b + (db % p.beam), p.beam),
            "comp": lax.rem(c + (dc % p.comp), p.comp),
        }

    def remote(source, target, send, recv, place):
        return pltpu.make_async_remote_copy(
            src_ref=source, dst_ref=target, send_sem=send, recv_sem=recv, device_id=place,
            device_id_type=MESH,
        )

    angle_load = pltpu.make_async_copy(angle_hbm, angle_ref, const_sem.at[7])
    angle_load.start()
    def columns_of(g, h):
        width = p.length // p.counts[g]
        return pl.ds(h * width, width)

    loads = []
    for h in range(PIECES):
        cols = columns_of(0, h)
        loads.append(
            pltpu.make_async_copy(raw_hbm.at[:, :, cols], raw.at[:, :, cols], load_sem.at[h])
        )
        loads[h].start()
    constants = [
        pltpu.make_async_copy(source, target, const_sem.at[i])
        for i, (source, target) in enumerate(
            [
                (weights_hbm, weights_ref), (offsets_hbm, offsets_ref), (delay_hbm, delay_ref),
                (first_hbm, first), (second_hbm, second), (turn_hbm, turn), (filter_hbm, filt),
            ]
        )
    ]
    for copy in constants:
        copy.start()

    window[:, 0] = jnp.zeros(window.shape[:1] + window.shape[2:], BF16)
    window[:, p.comp + 1] = jnp.zeros(window.shape[:1] + window.shape[2:], BF16)
    barrier = pltpu.get_barrier_semaphore()
    for place in p.peers:
        pl.semaphore_signal(barrier, inc=1, device_id=at(*place), device_id_type=MESH)

    angle_load.wait()
    angle = angle_ref[...]
    cos_part = (jnp.cos(angle) * p.factor).astype(BF16)
    sin_part = (jnp.sin(angle) * p.factor).astype(BF16)
    stacked = jnp.concatenate(
        [
            jnp.concatenate([cos_part, -sin_part], axis=1),
            jnp.concatenate([sin_part, cos_part], axis=1),
        ],
        axis=0,
    )
    count, deep = 2 * p.beams, 2 * p.pulses
    source = lax.broadcasted_iota(jnp.int32, (deep, deep), 0)
    target = lax.broadcasted_iota(jnp.int32, (deep, deep), 1)
    place = jnp.where(source < p.pulses, 2 * source, 2 * (source - p.pulses) + 1)
    spread = jnp.where(place == target, 1.0, 0.0).astype(BF16)
    target = lax.broadcasted_iota(jnp.int32, (count, count), 0)
    source = lax.broadcasted_iota(jnp.int32, (count, count), 1)

    def bits(value, size):
        return jnp.bitwise_and(value, size - 1), lax.shift_right_logical(
            value, jnp.full_like(value, size.bit_length() - 1)
        )

    def order_of(group_at, comp_at):
        return jnp.where(comp_at == p.comp - 1, p.groups - 1 - group_at, group_at)

    within, upper = bits(target, p.group)
    half, upper = bits(upper, 2)
    beam_at, upper = bits(upper, p.beam)
    comp_at, group_at = bits(upper, p.comp)
    group_at = order_of(group_at, comp_at)
    origin = half * p.beams + (
        (beam_at * p.comp + comp_at) * p.first + group_at * p.group + within
    )
    order = jnp.where(origin == source, 1.0, 0.0).astype(BF16)
    weight[...] = dot(order, dot(stacked, spread).astype(BF16)).astype(BF16)

    def table_copy(db, dc):
        slot = 1 + c if db == 0 else (0 if db > 0 else p.comp + 1)
        k = (db + 1) * p.comp + dc
        r = dc if db == 0 else (0 if db > 0 else p.comp)
        return remote(mine, tables.at[slot], table_send.at[k], table_recv.at[r], at(0, db, dc))

    def table_ends(action):
        @pl.when(c == p.comp - 1)
        def _():
            for e in range(p.comp):
                action(table_copy(1, e))

        @pl.when(c == 0)
        def _():
            for e in range(p.comp):
                action(table_copy(-1, e))

    def send_tables():
        for copy in constants[:3]:
            copy.wait()
        mine[...] = jnp.zeros(mine.shape, F32)
        for side in range(2):
            row = side * SIDE
            mine[row : row + BAND, : p.columns] = weights_ref[side]
            mine[row + BAND : row + BAND + 1, : p.columns] = offsets_ref[side : side + 1].astype(F32)
            mine[row + BAND + 1 : row + BAND + 2, : p.columns] = delay_ref[side : side + 1]
        tables[1 + c] = mine[...]
        for e in range(1, p.comp):
            table_copy(0, e).start()
        table_ends(lambda copy: copy.start())

    one, two, swaps = {}, {}, {}

    def bit(stage):
        return lax.rem(lax.div(b, 2**stage), 2)

    def form(h):
        loads[h].wait()
        cols = columns_of(0, h)
        pulses = raw[:, :, cols].reshape(2 * p.pulses, -1)
        product = dot(weight[...], pulses).astype(BF16)
        part[:, :, :, :, :, cols] = product.reshape(
            p.groups, p.comp, p.beam // 2, 2, p.rows, -1
        )

    def partner(stage):
        return {"beam": b + (1 - 2 * bit(stage)) * 2**stage}

    def start_one(g, h):
        if (g, h) in p.beam_first:
            n = p.beam_first.index((g, h))
            return send_wide(0, n, part.at[g, :, :, 1 - bit(0), :, columns_of(g, h)])
        one[g, h] = []
        for d in range(1, p.comp):
            peer = lax.rem(c + d, p.comp)
            k = p.units.index((g, h)) * (p.comp - 1) + d - 1
            copy = remote(
                part.at[g, peer, :, :, :, columns_of(g, h)],
                recv_one.at[d - 1, g, :, :, :, columns_of(g, h)],
                one_send.at[k], one_recv.at[k], at(0, 0, d),
            )
            copy.start()
            one[g, h].append(copy)

    def send_wide(stage, n, source):
        k = p.units.index(p.beam_first[n]) * p.stages + stage
        copy = remote(
            source, wide_recv[stage].at[n], two_send.at[k], two_recv.at[k], partner(stage)
        )
        copy.start()
        two[(stage,) + p.beam_first[n]] = copy

    def gathered_wide(stage, n):
        g, h = p.beam_first[n]
        two[stage, g, h].wait_recv()
        if stage == 0:
            total = part[g, :, :, bit(0), :, columns_of(g, h)].astype(F32)
        else:
            total = wide_held[stage][n, :, :, bit(stage)].astype(F32)
        return total + wide_recv[stage][n].astype(F32)

    def step_wide(stage, n):
        total = gathered_wide(stage - 1, n)
        if stage < p.stages:
            wide_held[stage][n] = total.astype(BF16).reshape(wide_held[stage].shape[1:])
            return send_wide(stage, n, wide_held[stage].at[n, :, :, 1 - bit(stage)])
        g, h = p.beam_first[n]
        late_held[n] = total[:, 0].astype(BF16)
        one[g, h] = []
        for d in range(1, p.comp):
            k = p.units.index((g, h)) * (p.comp - 1) + d - 1
            copy = remote(
                late_held.at[n, lax.rem(c + d, p.comp)], late_recv.at[n, d - 1],
                one_send.at[k], one_recv.at[k], at(0, 0, d),
            )
            copy.start()
            one[g, h].append(copy)

    def send_two(stage, g, h, total):
        cols = columns_of(g, h)
        held[stage][g, :, :, :, cols] = total.astype(BF16).reshape(-1, 2, p.rows, cols.size)
        k = p.units.index((g, h)) * p.stages + stage
        copy = remote(
            held[stage].at[g, :, 1 - bit(stage), :, cols],
            recv_two[stage].at[g, :, :, cols],
            two_send.at[k], two_recv.at[k], partner(stage),
        )
        copy.start()
        two[stage, g, h] = copy

    def gathered(stage, g, h):
        cols = columns_of(g, h)
        two[stage, g, h].wait_recv()
        total = held[stage][g, :, bit(stage), :, cols].astype(F32)
        return total + recv_two[stage][g, :, :, cols].astype(F32)

    def step_beam(stage, g, h):
        if (g, h) in p.beam_first:
            return step_wide(stage + 1, p.beam_first.index((g, h)))
        if stage > 0:
            return send_two(stage, g, h, gathered(stage - 1, g, h))
        cols = columns_of(g, h)
        for copy in one[g, h]:
            copy.wait_recv()
        total = part[g, c, :, :, :, cols].astype(F32)
        for d in range(1, p.comp):
            total += recv_one[d - 1, g, :, :, :, cols].astype(F32)
        send_two(0, g, h, total)

    def finish(g, h):
        if (g, h) in p.beam_first:
            n = p.beam_first.index((g, h))
            total = late_held[n, c].astype(F32)
            for copy in one[g, h]:
                copy.wait_recv()
            for d in range(1, p.comp):
                total += late_recv[n, d - 1].astype(F32)
        else:
            total = gathered(p.stages - 1, g, h)[0]
        width = p.length // p.counts[g]
        for a in range(width // radix):
            swap[pl.ds(h * (width // radix) + a, p.rows, stride=radix), :] = total[
                :, a * radix : (a + 1) * radix
            ]

    deferred = []

    def compress(g, deferring):
        factor = p.length ** (-0.5)
        h_real = filt[pl.ds(0, radix, stride=2), :] * factor
        h_imag = filt[pl.ds(1, radix, stride=2), :] * factor
        span = p.group * radix

        @pl.loop(0, p.group // 2)
        def _(pair):
            sides = []
            for u in range(2):
                row = pl.multiple_of((2 * pair + u) * radix, radix)
                sides.append(
                    jnp.concatenate(
                        [swap[pl.ds(row, radix), :], swap[pl.ds(row + span, radix), :]], axis=0
                    )
                )
            high, low = split(jnp.concatenate(sides, axis=1))
            section = dot(first[...], high) + dot(first[...], low)
            cos_turn, sin_turn = turn[0], turn[1]
            turned = []
            for u in range(2):
                real = section[:radix, u * radix : (u + 1) * radix]
                imag = section[radix:, u * radix : (u + 1) * radix]
                turned.append(
                    jnp.concatenate(
                        [
                            real * cos_turn - imag * sin_turn,
                            real * sin_turn + imag * cos_turn,
                        ],
                        axis=1,
                    )
                )
            high, low = split(jnp.concatenate(turned, axis=0))
            both_last = (((1,), (1,)), ((), ()))
            spectrum = lax.dot_general(second[...], high, both_last, preferred_element_type=F32)
            spectrum += lax.dot_general(second[...], low, both_last, preferred_element_type=F32)
            for u in range(2):
                real = spectrum[:radix, u * radix : (u + 1) * radix]
                imag = spectrum[radix:, u * radix : (u + 1) * radix]
                row = 2 * pair + u
                blend[pl.ds(row, radix, stride=p.rows), :] = real * h_real - imag * h_imag
                blend[pl.ds(row + p.group, radix, stride=p.rows), :] = (
                    real * h_imag + imag * h_real
                )

        image[g] = blend[...].reshape(radix, p.rows, radix).astype(BF16)
        window[s, 1 + c, g] = image[g, pl.ds((s * p.comp + c) * p.share, p.share)]
        number = OUT_PIECES if g == p.groups - 1 else 1
        size = p.share // number
        for o in range(number):
            swaps[g, o] = []
            for i, (ds, dc) in enumerate(p.swap_peers):
                where = at(ds, 0, dc)
                begin = (where["sub"] * p.comp + where["comp"]) * p.share + o * size
                k = (g + o) * len(p.swap_peers) + i
                copy = remote(
                    image.at[g, pl.ds(begin, size)],
                    window.at[s, 1 + c, g, pl.ds(o * size, size)],
                    swap_send.at[k], swap_recv.at[k], where,
                )
                swaps[g, o].append(copy)
                if dc == 0 or not deferring:
                    copy.start()
                else:
                    deferred.append(copy)

    def halo_copy(g, o, step):
        near, far = (1, p.comp + 1) if step < 0 else (p.comp, 0)
        size = p.share // (OUT_PIECES if g == p.groups - 1 else 1)
        k = 2 * (g + o) + (0 if step < 0 else 1)
        return remote(
            window.at[:, near, g, pl.ds(o * size, size)],
            window.at[:, far, g, pl.ds(o * size, size)],
            halo_send.at[k], halo_recv.at[k], {"beam": b + step},
        )

    def start_halo(g, o=0):
        for copy in swaps[g, o]:
            copy.wait_recv()
        if g not in p.edges:
            return

        @pl.when(has_low)
        def _():
            halo_copy(g, o, -1).start()

        @pl.when(has_high)
        def _():
            halo_copy(g, o, 1).start()

    def wait_halo(g, o=0):
        if g not in p.edges:
            return

        @pl.when(has_low)
        def _():
            halo_copy(g, o, 1).wait_recv()
            halo_copy(g, o, -1).wait_send()

        @pl.when(has_high)
        def _():
            halo_copy(g, o, -1).wait_recv()
            halo_copy(g, o, 1).wait_send()

    def read_tables():
        for e in range(1, p.comp):
            table_copy(0, e).wait_recv()
        table_copy(1, 0).wait_recv()
        table_copy(-1, 0).wait_recv()
        for j in range(p.padded // 128):
            block = tables[:, :, j * 128 : (j + 1) * 128].reshape(-1, 128)
            short = 128 - block.shape[0]
            if short > 0:
                block = jnp.concatenate([block, jnp.zeros((short, 128), F32)], axis=0)
            fields[j * 128 : (j + 1) * 128, :] = block.T

    def fields_of(level, side):
        for step, begin, size in p.pieces(level):
            row = p.first * (2 ** (level + 1) - 2) + begin
            yield step, size, row, (step + 1) * 2 * SIDE + side * SIDE

    def build(level):
        depth, size = p.depths[level], p.sizes[level]
        child = p.first * 2**level
        lane = lax.broadcasted_iota(jnp.int32, (1, depth), 1)
        if level == 0:
            within, upper = bits(lane, p.group)
            half, upper = bits(upper, 2)
            group_at, slot = bits(upper, p.groups)
            comp_at = jnp.where(slot == 0, p.comp - 1, jnp.where(slot > p.comp, 0, slot - 1))
            group_at = order_of(group_at, comp_at)
            beam_at = slot * p.first + group_at * p.group + within
        else:
            half = jnp.where(lane < depth // 2, 0, 1)
            beam_at = lane - half * (depth // 2)
        begin = p.first if level == 0 else EXTRA
        for side in range(2):
            done = 0
            for step, rows, row, base in fields_of(level, side):
                block = fields[row : row + rows, base : base + SIDE]
                shift = block[:, BAND : BAND + 1].astype(jnp.int32)
                tap = beam_at - begin - step * child - shift
                band = jnp.zeros((rows, depth), F32)
                for t in range(BAND):
                    band += jnp.where(tap == t, block[:, t : t + 1], 0.0)
                if step < 0:
                    band = jnp.where(has_low, band, 0.0)
                if step >= p.comp:
                    band = jnp.where(has_high, band, 0.0)
                for r in range(2):
                    high, low = split(jnp.where(half == r, band, 0.0))
                    lhs[level][side, 0, r * size + done : r * size + done + rows, :] = high
                    lhs[level][side, 1, r * size + done : r * size + done + rows, :] = low
                delay[level][side, done : done + rows, :] = jnp.broadcast_to(
                    block[:, BAND + 1 : BAND + 2], (rows, radix)
                )
                done += rows

    def build_phases(begin, end):
        start = (s * p.comp + c) * p.share

        @pl.loop(begin, end)
        def _(m):
            for level in range(levels):
                for side in range(2):
                    factor = delay[level][side]
                    lane = lax.broadcasted_iota(jnp.int32, factor.shape, 1)
                    place = ((start + m) * radix + lane).astype(F32)
                    phase_angle = factor * (1.0 + place / p.length)
                    phase[level][0, side, m] = jnp.cos(phase_angle)
                    phase[level][1, side, m] = jnp.sin(phase_angle)

    def merge(m):
        def pair(load):
            return jnp.concatenate([load(m), load(m + 1)], axis=1)

        images = [
            pair(lambda k, i=i: window[i, :, :, k].reshape(p.depths[0], radix))
            for i in range(p.sub)
        ]
        for level in range(levels):
            size = p.sizes[level]
            merged = []
            for g in range(len(images) // 2):
                real, imag = 0.0, 0.0
                for side in range(2):
                    child = images[2 * g + side]
                    mixed = dot(lhs[level][side, 0], child) + dot(lhs[level][side, 1], child)
                    cosine = pair(lambda k: phase[level][0, side, k])
                    sine = pair(lambda k: phase[level][1, side, k])
                    real += cosine * mixed[:size] - sine * mixed[size:]
                    imag += sine * mixed[:size] + cosine * mixed[size:]
                merged.append((real, imag))
            if level + 1 < levels:
                images = [jnp.concatenate(parts, axis=0).astype(BF16) for parts in merged]
        for r in range(2):
            for k in range(p.comp):
                for u in range(2):
                    value = merged[0][r][k * p.outs : (k + 1) * p.outs, u * radix : (u + 1) * radix]
                    final[k, m + u, r * p.outs : (r + 1) * p.outs, :] = value
                    outbound[k, m + u, r * p.outs : (r + 1) * p.outs, :] = value.astype(BF16)

    def place_out(source, m, column):
        for r in range(2):
            value = source[r * p.outs : (r + 1) * p.outs].astype(F32)
            out_ref[pl.ds(2 * (column * p.share + m) + r, p.outs, stride=2 * p.quarter), :] = value

    units = p.units
    total_units = len(units)
    idle = range(PIECES, 2 * PIECES)
    per_step = -(-p.share // len(idle))
    pending = []
    last = p.groups - 1
    drain = LAG + LAG_TWO * p.stages
    form(0)
    pl.semaphore_wait(barrier, len(p.peers))
    for u in range(total_units + drain):
        if 0 < u < PIECES:
            form(u)
        if u < total_units:
            start_one(*units[u])
        if u == 1:
            send_tables()
        if u == total_units - 1:
            for copy in deferred:
                copy.start()
        for stage in range(p.stages):
            v = u - LAG - LAG_TWO * stage
            if 0 <= v < total_units:
                step_beam(stage, *units[v])
        v = u - drain
        while pending and v >= pending[0][0]:
            start_halo(pending.pop(0)[1])
        if u == PIECES:
            read_tables()
            for copy in constants[3:]:
                copy.wait()
            for level in range(levels):
                build(level)
        if u in idle:
            begin = min((u - PIECES) * per_step, p.share)
            end = min(begin + per_step, p.share)
            if end > begin:
                build_phases(begin, end)
        if v >= 0:
            finish(*units[v])
            g, h = units[v]
            if h == p.counts[g] - 1:
                compress(g, u < total_units - 1)
                if g < last:
                    pending.append((max(v + HALO_LAG, total_units - drain + 4), g))
    for _, g in pending:
        start_halo(g)
    for g in range(last):
        wait_halo(g)

    chunk = p.share // OUT_PIECES
    outs = []

    def merge_piece(o):
        @pl.loop(0, chunk // 2)
        def _(i):
            merge(o * chunk + 2 * i)

        for d in range(1, p.comp):
            peer = lax.rem(c + d, p.comp)
            k = (d - 1) * OUT_PIECES + o
            copy = remote(
                outbound.at[peer, pl.ds(o * chunk, chunk)],
                inbound.at[d - 1, pl.ds(o * chunk, chunk)],
                out_send.at[k], out_recv.at[k], at(0, 0, d),
            )
            copy.start()
            outs.append((o, d, copy))

    for o in range(OUT_PIECES):
        start_halo(last, o)
        if last not in p.edges:
            merge_piece(o)
    if last in p.edges:
        for o in range(OUT_PIECES):
            wait_halo(last, o)
            merge_piece(o)

    @pl.loop(0, p.share)
    def _(m):
        place_out(final[c, m], m, c)

    for o, d, copy in outs:
        copy.wait_recv()
        origin = lax.rem(c + p.comp - d, p.comp)

        @pl.loop(0, chunk)
        def _(i, o=o, d=d, origin=origin):
            place_out(inbound[d - 1, o * chunk + i], o * chunk + i, origin)

    for e in range(1, p.comp):
        table_copy(0, e).wait_send()
    table_ends(lambda copy: copy.wait_send())
    for copy in itertools.chain(
        *one.values(), two.values(), *swaps.values(), (entry[2] for entry in outs)
    ):
        copy.wait_send()


def store_kernel(value_ref, out_hbm, sem):
    size = value_ref.shape[0] // STORES
    copies = [
        pltpu.make_async_copy(
            value_ref.at[pl.ds(i * size, size)], out_hbm.at[pl.ds(i * size, size)], sem.at[i]
        )
        for i in range(STORES)
    ]
    for copy in copies:
        copy.start()
    for copy in copies:
        copy.wait()


def store(value):
    return pl.pallas_call(
        store_kernel,
        out_shape=jax.ShapeDtypeStruct(value.shape, value.dtype),
        in_specs=[pl.BlockSpec(memory_space=pltpu.VMEM)],
        out_specs=pl.BlockSpec(memory_space=pl.ANY),
        scratch_shapes=[pltpu.SemaphoreType.DMA((STORES,))],
        compiler_params=pltpu.CompilerParams(vmem_limit_bytes=8 * 2**20),
    )(value)


def fused(plan, angle, raw, filt, weights, offsets, delay):
    p = plan
    constants = real_form(p.radix)
    dma = pltpu.SemaphoreType.DMA
    radix = p.radix
    units = len(p.units)
    wide = p.length // PIECES
    early = len(p.beam_first)
    halves = [p.beam // 2 ** (t + 1) for t in range(p.stages)]
    swap_count = p.groups - 1 + OUT_PIECES
    return pl.pallas_call(
        functools.partial(fused_kernel, p),
        out_shape=pltpu.VMEM((p.outs * 2 * p.quarter, radix), F32),
        in_specs=[pl.BlockSpec(memory_space=pltpu.HBM)] * 9,
        out_specs=pl.BlockSpec(memory_space=pltpu.VMEM),
        scratch_shapes=[
            pltpu.VMEM(angle.shape, F32),
            pltpu.VMEM(weights.shape, F32),
            pltpu.VMEM(offsets.shape, jnp.int32),
            pltpu.VMEM(delay.shape, F32),
            pltpu.VMEM(raw.shape, BF16),
            pltpu.VMEM((2 * p.beams, 2 * p.pulses), BF16),
            pltpu.VMEM((p.groups, p.comp, p.beam // 2, 2, p.rows, p.length), BF16),
            pltpu.VMEM((p.comp - 1, p.groups, p.beam // 2, 2, p.rows, p.length), BF16),
            pltpu.VMEM((p.rows * radix, radix), F32),
            pltpu.VMEM((2 * radix, 2 * radix), BF16),
            pltpu.VMEM((2 * radix, 2 * radix), BF16),
            pltpu.VMEM((2, radix, radix), F32),
            pltpu.VMEM((2 * radix, radix), F32),
            pltpu.VMEM((p.rows * radix, radix), F32),
            pltpu.VMEM((p.groups, radix, p.rows, radix), BF16),
            pltpu.VMEM((p.sub, p.slots, p.groups, p.share, p.rows, radix), BF16),
            pltpu.VMEM((2 * SIDE, p.padded), F32),
            pltpu.VMEM((p.slots, 2 * SIDE, p.padded), F32),
            pltpu.VMEM((p.padded, 128), F32),
            *[pltpu.VMEM((p.groups, n, 2, p.rows, p.length), BF16) for n in halves],
            *[pltpu.VMEM((p.groups, n, p.rows, p.length), BF16) for n in halves],
            *[
                pltpu.VMEM((early, p.comp, n if t else 1, 2, p.rows, wide if t else 128), BF16)
                for t, n in enumerate(halves)
            ],
            *[pltpu.VMEM((early, p.comp, n, p.rows, wide), BF16) for n in halves],
            pltpu.VMEM((early, p.comp, p.rows, wide), BF16),
            pltpu.VMEM((early, p.comp - 1, p.rows, wide), BF16),
            *[pltpu.VMEM((2, 2, 2 * n, k), BF16) for n, k in zip(p.sizes, p.depths)],
            *[pltpu.VMEM((2, n, radix), F32) for n in p.sizes],
            *[pltpu.VMEM((2, 2, p.share, n, radix), F32) for n in p.sizes],
            pltpu.VMEM((p.comp, p.share, 2 * p.outs, radix), F32),
            pltpu.VMEM((p.comp, p.share, 2 * p.outs, radix), BF16),
            pltpu.VMEM((p.comp - 1, p.share, 2 * p.outs, radix), BF16),
            dma((PIECES,)),
            dma((8,)),
            dma((3 * p.comp,)),
            dma((p.comp + 1,)),
            dma((units * (p.comp - 1),)),
            dma((units * (p.comp - 1),)),
            dma((units * p.stages,)),
            dma((units * p.stages,)),
            dma((swap_count * len(p.swap_peers),)),
            dma((swap_count * len(p.swap_peers),)),
            dma((2 * swap_count,)),
            dma((2 * swap_count,)),
            dma(((p.comp - 1) * OUT_PIECES,)),
            dma(((p.comp - 1) * OUT_PIECES,)),
        ],
        compiler_params=pltpu.CompilerParams(
            collective_id=0, has_side_effects=True, vmem_limit_bytes=LIMIT
        ),
    )(
        angle, raw, filt, weights, offsets, delay, jnp.asarray(constants.T), jnp.asarray(constants.T),
        jnp.asarray(twiddle(radix)),
    )


def body(raw_pulses, range_filter, steer_angle, band_offsets, band_weights, beam_delay):
    counts = (lax.axis_size("sub"), lax.axis_size("beam"), lax.axis_size("comp"))
    columns = band_offsets.shape[1]
    plan = Plan(counts, steer_angle.shape, raw_pulses.shape[2], columns)
    radix = plan.radix
    filt = range_filter.reshape(2, radix, radix).transpose(1, 0, 2).reshape(2 * radix, radix)
    out = fused(
        plan, steer_angle, raw_pulses, filt, band_weights.transpose(0, 2, 1), band_offsets, beam_delay
    )
    out = store(out)
    out = out.reshape(plan.outs, plan.quarter, 2, radix).transpose(0, 2, 1, 3)
    return out.reshape(plan.outs, 2, plan.quarter * radix)


def solution(mesh):
    in_specs = (
        P(("sub", "beam", "comp"), None, None),
        P(),
        P(None, ("sub", "beam", "comp")),
        P(None, ("beam", "comp")),
        P(None, ("beam", "comp"), None),
        P(None, ("beam", "comp")),
    )
    out_specs = P(("beam", "comp"), None, "sub")
    return jax.shard_map(body, mesh=mesh, in_specs=in_specs, out_specs=out_specs, check_vma=False)
```
